32 devices in a mesh: dp: 4 (over y, x), seq: 8 (over z, core).
Axes of the slice: x: 2, y: 2, z: 4, core: 2. Of those that a mesh axis runs over, the one named last changes fastest.
Arguments:
- video: bfloat16 [4, 32, 256, 768], P('dp', 'seq'), may hold values from -6 to 6
- space_qkv: bfloat16 [768, 2304], replicated, may hold values from -0.21875 to 0.21875
- space_out: bfloat16 [768, 768], replicated, may hold values from -0.21875 to 0.21875
- time_qkv: bfloat16 [768, 2304], replicated, may hold values from -0.21875 to 0.21875
- time_out: bfloat16 [768, 768], replicated, may hold values from -0.21875 to 0.21875
- proj_weight: bfloat16 [768, 128], replicated, may hold values from -0.21875 to 0.21875
- queries: bfloat16 [32, 32, 128], P('dp'), may hold values from -6 to 6
- query_len: int32 [32], P('dp'), may hold values from 1 to 32, 640 in all
- positive: int32 [32], P('dp'), may hold values from 0 to 3
Outputs:
- video_grad: bfloat16 [4, 32, 256, 128], P('dp', None, 'seq')
- query_grad: bfloat16 [32, 32, 128], P('dp')
- pair_loss: float32 [32, 4], P(None, 'dp')
The draws below stay inside these ranges and needn't reach their ends.
Inputs may be any that keep to these rules, and one draw needn't show every extreme that they name: `query_len`: the query lengths sum to 5 / 8 of all slots and the longest query fills all 32 slots.
All inputs are finite; a program needn't handle non-finite values. No bound on the sum of `query_len` on one device may be relied on, other than what follows from the above.
Results may differ from the reference program's by a relative error of at most 0.028.
Values may be sent and summed in bfloat16 or wider, within the bound.
A program may use at most 128 MiB of HBM per device.

```python
import math
import jax
import jax.numpy as jnp
import numpy as np
from jax import lax

D = 768
HEADS = 12
E = 128
P_SIZE = 256
LQ = 32
F = 32
V = 4
Q = 32


def touch_ends(drawn, stream_key, low, largest):
    shape = drawn.shape
    index_at = [jax.random.randint(jax.random.fold_in(stream_key, axis), (), 0, shape[axis]) for axis in range(len(shape))]
    drawn = drawn.at[tuple(index_at)].set(low)
    longest = shape.index(max(shape))
    index_at[longest] = (index_at[longest] + 1) % shape[longest]
    return drawn.at[tuple(index_at)].set(largest)


def levels(own_key, shape, shards, smallest, top_value):
    loudness = 1.0
    for position, shards_of in shards:
        heights = jax.random.uniform(jax.random.fold_in(jax.random.fold_in(own_key, 6), position), (shards_of,), jnp.float32, smallest / len(shards), top_value / len(shards))
        loudness = loudness * jnp.repeat(jnp.exp(heights), shape[position] // shards_of).reshape((-1,) + (1,) * (len(shape) - 1 - position))
    return loudness


def split_up(number_of, total, limit, skew):
    loads = [(1 << 20) // math.isqrt(grade ** skew) + 1 for grade in range(2, number_of + 1)]
    spare, given = total - limit - (number_of - 1), [1] * (number_of - 1)
    while spare > 0:
        movable = [i for i in range(number_of - 1) if given[i] < limit]
        whole, remaining = sum([loads[i] for i in movable]), spare
        for i in movable:
            addition = min(limit - given[i], max(1, remaining * loads[i] // whole), spare)
            given[i] = given[i] + addition
            spare = spare - addition
    return np.array([limit] + given)


def ragged_sizes(rng, count, total, limit, lean):
    if count == 2:
        one = jax.random.randint(rng, (), max(1, total - limit), min(limit, total - 1) + 1)
        return jnp.stack([one, total - one])
    sizes = jnp.asarray(split_up(count, total, limit, lean), jnp.int32)
    pairs = (count - 1) // 2
    source_of, taker = sizes[1:1 + 2 * pairs:2], sizes[2:2 + 2 * pairs:2]
    slack = jnp.minimum(source_of - 1, limit - taker)
    shifted = jax.random.randint(jax.random.fold_in(rng, 1), (pairs,), 0, 1 << 20) % (slack + 1)
    sizes = sizes.at[1:1 + 2 * pairs:2].set(source_of - shifted).at[2:2 + 2 * pairs:2].set(taker + shifted)
    return sizes[jax.random.permutation(jax.random.fold_in(rng, 2), count)]


def noise(stream_key, shape, scale, bound, split=(), kind=jnp.bfloat16):
    values = scale * jax.random.normal(stream_key, shape, jnp.float32)
    if split:
        values = values * levels(stream_key, shape, split, -0.22, 0.18)
    return jnp.clip(values, -bound, bound).astype(kind)


def setup_inputs(seed: int = 0) -> dict:
    arg_keys = jax.random.split(jax.random.key(seed), 10)
    return {
        "video": noise(arg_keys[0], (V, F, P_SIZE, D), 1.0, 6.0, ((0, 4), (1, 8))),
        "space_qkv": noise(arg_keys[1], (D, 3 * D), D ** -0.5, 0.21875),
        "space_out": noise(arg_keys[2], (D, D), D ** -0.5, 0.21875),
        "time_qkv": noise(arg_keys[3], (D, 3 * D), D ** -0.5, 0.21875),
        "time_out": noise(arg_keys[4], (D, D), D ** -0.5, 0.21875),
        "proj_weight": noise(arg_keys[5], (D, E), D ** -0.5, 0.21875),
        "queries": noise(arg_keys[6], (Q, LQ, E), 1.0, 6.0, ((0, 4),)),
        "query_len": ragged_sizes(arg_keys[7], Q, Q * LQ * 5 // 8, LQ, 1).astype(jnp.int32),
        "positive": touch_ends(jax.random.randint(arg_keys[8], (Q,), 0, V), jax.random.fold_in(arg_keys[8], 1), 0, V - 1).astype(jnp.int32),
    }


TEMPER = 0.05
SLOPE = 10.0
OFFSET = -5.0
SHARP = 10.0

def layer_norm(tokens):
    values = tokens.astype(jnp.float32)
    center = values - lax.optimization_barrier(jnp.mean(values, axis=-1, keepdims=True))
    spread = lax.optimization_barrier(jnp.mean(center * center, axis=-1, keepdims=True))
    return (center / jnp.sqrt(spread + 1e-05)).astype(jnp.bfloat16)

def unit_rows(values):
    values = values.astype(jnp.float32)
    return values / jnp.sqrt(lax.optimization_barrier(jnp.sum(values * values, axis=-1, keepdims=True)) + 1e-06)

def attend(tokens, qkv_weight, out_weight):
    groups, extent, feature = tokens.shape
    normed = layer_norm(tokens)
    packed = jnp.einsum('nld,de->nle', normed.astype(jnp.float32), qkv_weight.astype(jnp.float32)).astype(jnp.bfloat16)
    packed = packed.reshape(groups, extent, 3, HEADS, feature // HEADS)
    query_rows = unit_rows(packed[:, :, 0]).astype(jnp.bfloat16)
    key_rows = unit_rows(packed[:, :, 1]).astype(jnp.bfloat16)
    scores = jnp.einsum('nqhc,nkhc->nhqk', query_rows.astype(jnp.float32), key_rows.astype(jnp.float32))
    weights = jnp.exp(SHARP * scores)
    weights = (weights / lax.optimization_barrier(jnp.sum(weights, axis=-1, keepdims=True))).astype(jnp.bfloat16)
    blended = jnp.einsum('nhqk,nkhc->nqhc', weights.astype(jnp.float32), packed[:, :, 2].astype(jnp.float32))
    blended = blended.astype(jnp.bfloat16).reshape(groups, extent, feature)
    update = jnp.einsum('nld,de->nle', blended.astype(jnp.float32), out_weight.astype(jnp.float32))
    return (tokens.astype(jnp.float32) + update).astype(jnp.bfloat16)

def reference(video, space_qkv, space_out, time_qkv, time_out, proj_weight, queries, query_len, positive):

    def encode(one_video):
        spatial = attend(one_video, space_qkv, space_out)
        columns = jnp.transpose(spatial, (1, 0, 2))
        mixed_cols = attend(columns, time_qkv, time_out)
        projected = jnp.dot(layer_norm(mixed_cols).reshape(-1, D), proj_weight, preferred_element_type=jnp.float32)
        embedded = unit_rows(projected).astype(jnp.bfloat16).reshape(P_SIZE, F, E)
        return jnp.transpose(embedded, (1, 0, 2)).reshape(F * P_SIZE, E)
    token_emb = lax.map(encode, video)
    unit_query = unit_rows(queries).astype(jnp.bfloat16).reshape(Q * LQ, E)

    def video_sums(key_rows):
        dot_raw = jnp.dot(unit_query, key_rows.T, preferred_element_type=jnp.float32)
        return lax.optimization_barrier(jnp.sum(jnp.exp((dot_raw - 1.0) / TEMPER), axis=-1))
    totals = lax.map(video_sums, token_emb)
    smooth = (1.0 + TEMPER * jnp.log(totals)).T.reshape(Q, LQ, V)
    token_mask = (jnp.arange(LQ, dtype=jnp.int32)[None, :] < query_len[:, None]).astype(jnp.float32)
    token_count = query_len.astype(jnp.float32)
    scores_pair = lax.optimization_barrier(jnp.sum(smooth * token_mask[:, :, None], axis=1)) / token_count[:, None]
    pair_sign = jnp.where(positive[:, None] == jnp.arange(V, dtype=jnp.int32)[None, :], 1.0, -1.0)
    margin = pair_sign * (SLOPE * scores_pair + OFFSET)
    pair_loss = jax.nn.softplus(-margin)
    pair_grad = -pair_sign * SLOPE * jax.nn.sigmoid(-margin)
    token_coeff = pair_grad[:, None, :] * (token_mask / token_count[:, None])[:, :, None]
    coeff_rows = token_coeff.reshape(Q * LQ, V).T

    def video_grads(running, inputs):
        key_rows, row_total, weight = inputs
        dot_raw = jnp.dot(unit_query, key_rows.T, preferred_element_type=jnp.float32)
        expo_terms = jnp.exp((dot_raw - 1.0) / TEMPER)
        weights_bf = (expo_terms / row_total[:, None] * weight[:, None]).astype(jnp.bfloat16)
        key_grad = jnp.dot(weights_bf.T, unit_query, preferred_element_type=jnp.float32)
        return (running + jnp.dot(weights_bf, key_rows, preferred_element_type=jnp.float32), key_grad)
    query_total, key_grads = lax.scan(video_grads, jnp.zeros((Q * LQ, E), jnp.float32), (token_emb, totals, coeff_rows))
    video_grad = (F * P_SIZE * key_grads).astype(jnp.bfloat16).reshape(V, F, P_SIZE, E)
    query_grad = (LQ * query_total).astype(jnp.bfloat16).reshape(Q, LQ, E)
    return (video_grad, query_grad, pair_loss)
```

```python
import functools

import jax
import jax.numpy as jnp
from jax import lax
from jax.experimental import pallas as pl
from jax.experimental.pallas import tpu as pltpu
from jax.sharding import PartitionSpec as P

HEADS = 12
TEMPER = 0.05
SLOPE = 10.0
OFFSET = -5.0
SHARP = 10.0
CHUNK = 256
PG = 8
F32 = jnp.float32
BF16 = jnp.bfloat16


def dot(a, b):
    return jnp.dot(a, b, preferred_element_type=F32)


def dot_nt(a, b):
    return lax.dot_general(a, b, (((1,), (1,)), ((), ())), preferred_element_type=F32)


def dot_tn(a, b):
    return lax.dot_general(a, b, (((0,), (0,)), ((), ())), preferred_element_type=F32)


def layer_norm(values):
    center = values - jnp.mean(values, axis=-1, keepdims=True)
    spread = jnp.mean(center * center, axis=-1, keepdims=True)
    return (center * lax.rsqrt(spread + 1e-05)).astype(BF16)


def head_unit(values, same_head, scale):
    total = dot((values * values).astype(BF16), same_head)
    return values * (lax.rsqrt(total + 1e-06) * scale)


def blend(qn, kn, v, low, high, mask):
    rows = qn.shape[0]
    lane = lax.broadcasted_iota(jnp.int32, (rows, 128), 1) < 64
    ones = jnp.ones((rows, 128), BF16)
    out = []
    for p in range(CHUNK // 128):
        cols = slice(128 * p, 128 * p + 128)
        kp = kn[:, cols]
        vx = jnp.concatenate([v[:, cols], ones], axis=1)
        res = []
        for half in (low, high):
            e = jnp.exp(dot_nt(qn[:, cols] * half, kp)).astype(BF16)
            if mask is not None:
                e = e * mask
            res.append(dot(e, vx))
        num = jnp.where(lane, res[0][:, :128], res[1][:, :128])
        den = jnp.where(lane, res[0][:, 128:], res[1][:, 128:])
        out.append((num / den).astype(BF16))
    return jnp.concatenate(out, axis=1)


def kernel(
    nd, ns, lq,
    video, w_sq, w_so, w_tq, w_to, w_p, queries, qlen, qpos,
    vg, qg, loss,
    vbuf, sq, so, tq, to, pw, obuf, bl, recv, bl2, mask, kh, ebuf, sums, qs,
    qall, meta, srecv, part, prec, zrec, gath, qht,
    in_sem, w_sem, as_sem, ar_sem, bs_sem, br_sem, qs_sem, qr_sem, ms_sem, mr_sem, ss_sem, sr_sem,
    ps_sem, pr_sem, rs_sem, rr_sem, gs_sem, gr_sem,
):
    frames, patches, width = vbuf.shape
    ploc = patches // ns
    fall = frames * ns
    rows = fall * PG
    groups = ploc // PG
    chunks = width // CHUNK
    qb = qall.shape[1]
    qt = nd * qb
    mrows = qb // 128
    me_d = lax.axis_index("dp")
    me_s = lax.axis_index("seq")

    def ahead(axis, k):
        if axis == "dp":
            return lax.rem(me_d + k, nd)
        peer, bit = 0, 1
        while bit < ns:
            digit = (me_s // bit) % 2
            peer = peer + bit * (1 - digit if k & bit else digit)
            bit *= 2
        return peer

    def remote(src, dst, send, recv_at, axis, peer):
        return pltpu.make_async_remote_copy(
            src_ref=src, dst_ref=dst, send_sem=send, recv_sem=recv_at,
            device_id={axis: peer}, device_id_type=pl.DeviceIdType.MESH,
        )

    pairs = []
    for c in range(chunks):
        for third in range(3):
            cols = pl.ds(third * width + CHUNK * c, CHUNK)
            pairs.append((w_sq.at[:, cols], sq.at[:, cols]))
    first = len(pairs)
    pairs += [(w_so, so), (w_tq, tq), (w_to, to), (w_p, pw)]
    loads = [
        pltpu.make_async_copy(src, dst, w_sem.at[i]) for i, (src, dst) in enumerate(pairs)
    ]

    def frame_load(f):
        return pltpu.make_async_copy(video.at[0, f], vbuf.at[f], in_sem.at[f])

    frame_load(0).start()
    for i in range(first + 1):
        loads[i].start()
    for f in range(1, frames):
        frame_load(f).start()
    for i in range(first + 1, first + 4):
        loads[i].start()

    barrier = pltpu.get_barrier_semaphore()
    for k in range(1, ns):
        pl.semaphore_signal(
            barrier, inc=1, device_id={"seq": ahead("seq", k)},
            device_id_type=pl.DeviceIdType.MESH,
        )
    for k in range(1, nd):
        for c in range(2):
            pl.semaphore_signal(
                barrier, inc=1, device_id={"dp": ahead("dp", k), "seq": ahead("seq", c)},
                device_id_type=pl.DeviceIdType.MESH,
            )

    lane128 = lax.broadcasted_iota(jnp.int32, (1, 128), 1)
    low = (lane128 < 64).astype(F32).astype(BF16)
    high = (lane128 >= 64).astype(F32).astype(BF16)
    ra = lax.broadcasted_iota(jnp.int32, (CHUNK, CHUNK), 0) // 64
    ca = lax.broadcasted_iota(jnp.int32, (CHUNK, CHUNK), 1) // 64
    same_head = (ra == ca).astype(F32).astype(BF16)
    rm = lax.broadcasted_iota(jnp.int32, (rows, rows), 0) % PG
    cm = lax.broadcasted_iota(jnp.int32, (rows, rows), 1) % PG
    mask[...] = (rm == cm).astype(F32).astype(BF16)

    per = 128 // lq
    tile = []
    for source in (qlen, qpos):
        for r in range(mrows):
            row = jnp.zeros((1, 128), jnp.int32)
            for c in range(per):
                row = jnp.where(lane128 // lq == c, source[r * per + c], row)
            tile.append(row)
    tile.append(jnp.zeros((8 - 2 * mrows, 128), jnp.int32))
    meta[me_d] = jnp.concatenate(tile, axis=0)
    qall[me_d] = queries[...]

    def query_copy(k):
        return remote(queries, qall.at[me_d], qs_sem.at[k - 1], qr_sem.at[k - 1], "dp", ahead("dp", k))

    def meta_copy(k):
        return remote(meta.at[me_d], meta.at[me_d], ms_sem.at[k - 1], mr_sem.at[k - 1], "dp", ahead("dp", k))

    lead = max(1, groups // 2)
    order = range(1, ns)

    def rows_copy(f, k):
        peer = ahead("seq", k)
        return remote(
            obuf.at[f, pl.ds(peer * groups, lead)], recv.at[pl.ds(0, lead), me_s, f],
            as_sem.at[f, k - 1], ar_sem.at[f, k - 1], "seq", peer,
        )

    def group_copy(g, k):
        peer = ahead("seq", k)
        return remote(
            obuf.at[:, peer * groups + g], recv.at[g, me_s],
            bs_sem.at[g - lead, k - 1], br_sem.at[g - lead, k - 1], "seq", peer,
        )

    def spatial(f, first_time):
        frame_load(f).wait()
        normed = layer_norm(vbuf[f].astype(F32))
        for c in range(chunks):
            at = CHUNK * c
            if first_time:
                for third in range(3):
                    loads[3 * c + third].wait()
            q = dot(normed, sq[:, at:at + CHUNK])
            k = dot(normed, sq[:, width + at:width + at + CHUNK])
            v = dot(normed, sq[:, 2 * width + at:2 * width + at + CHUNK]).astype(BF16)
            qn = head_unit(q, same_head, SHARP).astype(BF16)
            kn = head_unit(k, same_head, 1.0).astype(BF16)
            bl[:, at:at + CHUNK] = blend(qn, kn, v, low, high, None)

    def spatial_out(f):
        for c in range(chunks):
            at = CHUNK * c
            update = dot(bl[...], so[:, at:at + CHUNK])
            obuf[f, :, :, at:at + CHUNK] = (
                vbuf[f, :, at:at + CHUNK].astype(F32) + update
            ).astype(BF16).reshape(patches // PG, PG, CHUNK)
        for k in order:
            rows_copy(f, k).start()

    spatial(0, True)
    loads[first].wait()
    pl.semaphore_wait(barrier, 2 * (nd - 1) + ns - 1)
    spatial_out(0)
    for k in range(1, nd):
        query_copy(k).start()
    for k in range(1, nd):
        meta_copy(k).start()

    @pl.loop(1, frames)
    def _(f):
        spatial(f, False)
        spatial_out(f)

    for g in range(lead, groups):
        for k in order:
            group_copy(g, k).start()
    for g in range(groups):
        recv[g, me_s] = obuf[:, me_s * groups + g]

    for k in range(1, nd):
        query_copy(k).wait()
        meta_copy(k).wait()
    for d in range(nd):
        qf = qall[d].astype(F32).T
        norm = lax.rsqrt(jnp.sum(qf * qf, axis=0, keepdims=True) + 1e-06)
        qht[:, d * qb:(d + 1) * qb] = (qf * norm).astype(BF16)
    sums[...] = jnp.zeros_like(sums)
    qs[...] = jnp.zeros_like(qs)
    for i in range(first + 1, first + 4):
        loads[i].wait()
    for f in range(frames):
        for k in order:
            rows_copy(f, k).wait_recv()

    @pl.loop(0, groups)
    def _(g):
        @pl.when(g >= lead)
        def _():
            for k in order:
                group_copy(g, k).wait_recv()

        x = recv[g].astype(F32).reshape(rows, width)
        normed = layer_norm(x)
        for c in range(chunks):
            at = CHUNK * c
            q = dot(normed, tq[:, at:at + CHUNK])
            k = dot(normed, tq[:, width + at:width + at + CHUNK])
            v = dot(normed, tq[:, 2 * width + at:2 * width + at + CHUNK]).astype(BF16)
            qn = head_unit(q, same_head, SHARP).astype(BF16)
            kn = head_unit(k, same_head, 1.0).astype(BF16)
            bl2[:, at:at + CHUNK] = blend(qn, kn, v, low, high, mask[...])
        mixed = x + dot(bl2[...], to[...])
        normed = layer_norm(mixed.astype(BF16).astype(F32))
        proj = dot(normed, pw[...])
        key = (proj * lax.rsqrt(jnp.sum(proj * proj, axis=-1, keepdims=True) + 1e-06)).astype(BF16)
        kh[g] = key
        for c in range(qt // CHUNK):
            cols = slice(CHUNK * c, CHUNK * c + CHUNK)
            e = jnp.exp((dot(key, qht[:, cols]) - 1.0) * (1.0 / TEMPER))
            sums[:, cols] += jnp.sum(e, axis=0, keepdims=True)
            eb = e.astype(BF16)
            ebuf[g, :, cols] = eb
            qs[:, cols] += dot_tn(key, eb)

    for r in range(qt // 128):
        srecv[me_s, r:r + 1, :] = sums[:, 128 * r:128 * r + 128]

    def sums_copy(k):
        return remote(srecv.at[me_s], srecv.at[me_s], ss_sem.at[k - 1], sr_sem.at[k - 1], "seq", ahead("seq", k))

    for k in range(1, ns):
        sums_copy(k).start()
    for k in range(1, ns):
        sums_copy(k).wait()
    total = srecv[0]
    for s in range(1, ns):
        total = total + srecv[s]

    all_len = jnp.concatenate([meta[d, :mrows] for d in range(nd)], axis=0)
    all_pos = jnp.concatenate([meta[d, mrows:2 * mrows] for d in range(nd)], axis=0)
    trows = qt // 128
    slot = lax.broadcasted_iota(jnp.int32, (trows, 128), 1) % lq
    valid = (slot < all_len).astype(F32)
    count = all_len.astype(F32)
    seg_a = lax.broadcasted_iota(jnp.int32, (128, 128), 0) // lq
    seg_b = lax.broadcasted_iota(jnp.int32, (128, 128), 1) // lq
    seg = (seg_a == seg_b).astype(F32)
    smooth = (1.0 + TEMPER * jnp.log(total)) * valid
    score = jnp.dot(smooth, seg, precision=lax.Precision.HIGHEST, preferred_element_type=F32) / count
    sign = jnp.where(all_pos == me_d, 1.0, -1.0)
    margin = sign * (SLOPE * score + OFFSET)
    tail = jnp.exp(-jnp.abs(margin))
    losses = jnp.maximum(-margin, 0.0) + jnp.log1p(tail)
    coeff = -sign * SLOPE / (1.0 + jnp.exp(margin)) * valid / count
    scale = coeff / total
    nq = qt // lq
    lr = lax.broadcasted_iota(jnp.int32, (128, nq), 0)
    lc = lax.broadcasted_iota(jnp.int32, (128, nq), 1)
    pick = (lr == lc % per * lq).astype(F32)
    spread = jnp.dot(losses, pick, precision=lax.Precision.HIGHEST, preferred_element_type=F32)
    qr = lax.broadcasted_iota(jnp.int32, (trows, nq), 0)
    qc = lax.broadcasted_iota(jnp.int32, (trows, nq), 1) // per
    loss[...] = jnp.sum(jnp.where(qr == qc, spread, 0.0), axis=0, keepdims=True)

    wrow = jnp.concatenate([scale[r:r + 1] for r in range(trows)], axis=1)
    for d in range(nd):
        cols = slice(d * qb, (d + 1) * qb)
        part[d] = (qs[:, cols] * wrow[:, cols]).T.astype(BF16).reshape(2, qb // 2, 128)
    me_c = me_s % 2
    me_z = me_s // 2
    prec[me_d, me_c] = part[me_d, me_c]
    near = [(k, c) for k in range(nd) for c in range(2) if k + c > 0]

    def part_copy(i):
        k, c = near[i]
        peer_d = ahead("dp", k)
        peer_s = ahead("seq", c)
        return pltpu.make_async_remote_copy(
            src_ref=part.at[peer_d, peer_s % 2], dst_ref=prec.at[me_d, me_c],
            send_sem=ps_sem.at[i], recv_sem=pr_sem.at[i],
            device_id={"dp": peer_d, "seq": peer_s}, device_id_type=pl.DeviceIdType.MESH,
        )

    for i in range(len(near)):
        part_copy(i).start()

    wq = (qht[...].astype(F32) * wrow).astype(BF16)
    for b in range(ploc // 16):
        halves = [
            (dot_nt(ebuf[2 * b + h], wq) * float(fall * patches)).reshape(fall, PG, 128)
            for h in range(2)
        ]
        vg[0, :, 16 * b:16 * b + 16, :] = jnp.concatenate(halves, axis=1).astype(BF16)

    for i in range(len(near)):
        part_copy(i).wait()
    acc = jnp.zeros((qb // 2, 128), F32)
    for d in range(nd):
        for c in range(2):
            acc = acc + prec[d, c].astype(F32)
    zrec[me_z] = acc.astype(BF16)

    def chip_copy(k):
        return remote(zrec.at[me_z], zrec.at[me_z], rs_sem.at[k - 1], rr_sem.at[k - 1], "seq", ahead("seq", 2 * k))

    for k in range(ns // 2 - 1, 0, -1):
        chip_copy(k).start()
    for k in range(1, ns // 2):
        chip_copy(k).wait()
    acc = zrec[0].astype(F32)
    for z in range(1, ns // 2):
        acc = acc + zrec[z].astype(F32)
    gath[me_c] = (acc * float(lq)).astype(BF16)
    swap = remote(gath.at[me_c], gath.at[me_c], gs_sem.at[0], gr_sem.at[0], "seq", ahead("seq", 1))
    swap.start()
    swap.wait()
    qg[...] = gath[...].reshape(qg.shape)

    @pl.loop(0, frames)
    def _(f):
        for k in range(1, ns):
            rows_copy(f, k).wait_send()

    for g in range(lead, groups):
        for k in order:
            group_copy(g, k).wait_send()


def finish(vg_in, qg_in, loss_in, vg_out, qg_out, loss_out):
    vg_out[...] = vg_in[...]
    qg_out[...] = qg_in[...]
    loss_out[...] = loss_in[...]


def body(nd, ns, video, space_qkv, space_out, time_qkv, time_out, proj_weight, queries, query_len, positive):
    videos_dev, frames, patches, width = video.shape
    assert videos_dev == 1
    qdev, lq, embed = queries.shape
    ploc = patches // ns
    fall = frames * ns
    rows = fall * PG
    groups = ploc // PG
    qb = qdev * lq
    qt = nd * qb
    vmem = pltpu.VMEM
    dma = pltpu.SemaphoreType.DMA
    anyspec = pl.BlockSpec(memory_space=pl.ANY)
    vspec = pl.BlockSpec(memory_space=pltpu.VMEM)
    sspec = pl.BlockSpec(memory_space=pltpu.SMEM)
    vg, qg, loss = pl.pallas_call(
        functools.partial(kernel, nd, ns, lq),
        out_shape=(
            jax.ShapeDtypeStruct((1, fall, ploc, embed), BF16),
            jax.ShapeDtypeStruct((qdev, lq, embed), BF16),
            jax.ShapeDtypeStruct((1, nd * qdev), F32),
        ),
        in_specs=[anyspec] * 6 + [vspec, sspec, sspec],
        out_specs=(vspec, vspec, vspec),
        scratch_shapes=[
            vmem((frames, patches, width), BF16),
            vmem(space_qkv.shape, BF16),
            vmem(space_out.shape, BF16),
            vmem(time_qkv.shape, BF16),
            vmem(time_out.shape, BF16),
            vmem(proj_weight.shape, BF16),
            vmem((frames, patches // PG, PG, width), BF16),
            vmem((patches, width), BF16),
            vmem((groups, ns, frames, PG, width), BF16),
            vmem((rows, width), BF16),
            vmem((rows, rows), BF16),
            vmem((groups, rows, embed), BF16),
            vmem((groups, rows, qt), BF16),
            vmem((1, qt), F32),
            vmem((embed, qt), F32),
            vmem((nd, qb, embed), BF16),
            vmem((nd, 8, 128), jnp.int32),
            vmem((ns, qt // 128, 128), F32),
            vmem((nd, 2, qb // 2, embed), BF16),
            vmem((nd, 2, qb // 2, embed), BF16),
            vmem((ns // 2, qb // 2, embed), BF16),
            vmem((2, qb // 2, embed), BF16),
            vmem((embed, qt), BF16),
            dma((frames,)), dma((3 * (width // CHUNK) + 4,)),
            dma((frames, ns - 1)), dma((frames, ns - 1)),
            dma((max(1, groups - groups // 2), ns - 1)), dma((max(1, groups - groups // 2), ns - 1)),
            dma((nd - 1,)), dma((nd - 1,)),
            dma((nd - 1,)), dma((nd - 1,)),
            dma((ns - 1,)), dma((ns - 1,)),
            dma((2 * nd - 1,)), dma((2 * nd - 1,)),
            dma((ns // 2 - 1,)), dma((ns // 2 - 1,)),
            dma((1,)), dma((1,)),
        ],
        compiler_params=pltpu.CompilerParams(
            collective_id=0, has_side_effects=True, vmem_limit_bytes=60 * 1024 * 1024
        ),
    )(
        video, space_qkv, space_out, time_qkv, time_out, proj_weight,
        queries.reshape(qb, embed), query_len, positive,
    )
    vg, qg, loss = pl.pallas_call(
        finish,
        out_shape=(
            jax.ShapeDtypeStruct(vg.shape, BF16),
            jax.ShapeDtypeStruct(qg.shape, BF16),
            jax.ShapeDtypeStruct(loss.shape, F32),
        ),
        in_specs=[vspec] * 3,
        out_specs=(vspec, vspec, vspec),
    )(vg, qg, loss)
    return vg, qg, loss.reshape(nd * qdev, 1)


def solution(mesh):
    nd, ns = mesh.shape["dp"], mesh.shape["seq"]
    placed = (
        P("dp", "seq", None, None),
        P(), P(), P(), P(), P(),
        P("dp", None, None),
        P("dp"),
        P("dp"),
    )
    return jax.shard_map(
        functools.partial(body, nd, ns),
        mesh=mesh,
        in_specs=placed,
        out_specs=(P("dp", None, "seq", None), P("dp", None, None), P(None, "dp")),
        check_vma=False,
    )
```

```python
import functools

import jax
import jax.numpy as jnp
from jax import lax
from jax.experimental import pallas as pl
from jax.experimental.pallas import tpu as pltpu
from jax.sharding import PartitionSpec as P

HEADS = 12
TEMPER = 0.05
SLOPE = 10.0
OFFSET = -5.0
SHARP = 10.0
CHUNK = 256
PG = 8
F32 = jnp.float32
BF16 = jnp.bfloat16


def dot(a, b):
    return jnp.dot(a, b, preferred_element_type=F32)


def dot_nt(a, b):
    return lax.dot_general(a, b, (((1,), (1,)), ((), ())), preferred_element_type=F32)


def dot_tn(a, b):
    return lax.dot_general(a, b, (((0,), (0,)), ((), ())), preferred_element_type=F32)


def layer_norm(values):
    center = values - jnp.mean(values, axis=-1, keepdims=True)
    spread = jnp.mean(center * center, axis=-1, keepdims=True)
    return (center * lax.rsqrt(spread + 1e-05)).astype(BF16)


def head_unit(values, same_head, scale):
    total = dot((values * values).astype(BF16), same_head)
    return values * (lax.rsqrt(total + 1e-06) * scale)


def blend(qn, kn, v, low, high, mask):
    rows = qn.shape[0]
    lane = lax.broadcasted_iota(jnp.int32, (rows, 128), 1) < 64
    ones = jnp.ones((rows, 128), BF16)
    out = []
    for p in range(CHUNK // 128):
        cols = slice(128 * p, 128 * p + 128)
        kp = kn[:, cols]
        vx = jnp.concatenate([v[:, cols], ones], axis=1)
        res = []
        for half in (low, high):
            e = jnp.exp(dot_nt(qn[:, cols] * half, kp)).astype(BF16)
            if mask is not None:
                e = e * mask
            res.append(dot(e, vx))
        num = jnp.where(lane, res[0][:, :128], res[1][:, :128])
        den = jnp.where(lane, res[0][:, 128:], res[1][:, 128:])
        out.append((num / den).astype(BF16))
    return jnp.concatenate(out, axis=1)


def kernel(
    nd, ns, lq,
    video, w_sq, w_so, w_tq, w_to, w_p, queries, qlen_in, qpos_in,
    vg, qg, loss,
    vbuf, sq, so, tq, to, pw, obuf, bl, recv, bl2, mask, kh, ebuf, sums, qs,
    qall, meta, srecv, xrecv, part, prec, zrec, gath, qht, vgbuf, qlen, qpos,
    in_sem, w_sem, q_sem, v_sem, as_sem, ar_sem, bs_sem, br_sem, qs_sem, qr_sem, ms_sem, mr_sem, ss_sem, sr_sem,
    xs_sem, xr_sem, ps_sem, pr_sem, rs_sem, rr_sem, gs_sem, gr_sem,
):
    frames, patches, width = vbuf.shape
    ploc = patches // ns
    fall = frames * ns
    rows = fall * PG
    groups = ploc // PG
    chunks = width // CHUNK
    qb = qall.shape[1]
    qt = nd * qb
    mrows = qb // 128
    me_d = lax.axis_index("dp")
    me_s = lax.axis_index("seq")

    def ahead(axis, k):
        if axis == "dp":
            return lax.rem(me_d + k, nd)
        peer, bit = 0, 1
        while bit < ns:
            digit = (me_s // bit) % 2
            peer = peer + bit * (1 - digit if k & bit else digit)
            bit *= 2
        return peer

    def remote(src, dst, send, recv_at, axis, peer):
        return pltpu.make_async_remote_copy(
            src_ref=src, dst_ref=dst, send_sem=send, recv_sem=recv_at,
            device_id={axis: peer}, device_id_type=pl.DeviceIdType.MESH,
        )

    pairs = []
    for c in range(chunks):
        for third in range(3):
            cols = pl.ds(third * width + CHUNK * c, CHUNK)
            pairs.append((w_sq.at[:, cols], sq.at[:, cols]))
    first = len(pairs)
    pairs += [(w_so, so), (w_tq, tq), (w_to, to), (w_p, pw)]
    loads = [
        pltpu.make_async_copy(src, dst, w_sem.at[i]) for i, (src, dst) in enumerate(pairs)
    ]

    def frame_load(f):
        return pltpu.make_async_copy(video.at[0, f], vbuf.at[f], in_sem.at[f])

    query_loads = [
        pltpu.make_async_copy(queries, qall.at[me_d], q_sem.at[0]),
        pltpu.make_async_copy(qlen_in, qlen, q_sem.at[1]),
        pltpu.make_async_copy(qpos_in, qpos, q_sem.at[2]),
    ]
    frame_load(0).start()
    for i in range(first + 1):
        loads[i].start()
    for load in query_loads:
        load.start()
    for f in range(1, frames):
        frame_load(f).start()
    for i in range(first + 1, first + 4):
        loads[i].start()

    barrier = pltpu.get_barrier_semaphore()
    others = [(k, c) for k in range(nd) for c in range(ns) if k + c > 0]
    for k, c in others:
        pl.semaphore_signal(
            barrier, inc=1, device_id={"dp": ahead("dp", k), "seq": ahead("seq", c)},
            device_id_type=pl.DeviceIdType.MESH,
        )

    lane128 = lax.broadcasted_iota(jnp.int32, (1, 128), 1)
    low = (lane128 < 64).astype(F32).astype(BF16)
    high = (lane128 >= 64).astype(F32).astype(BF16)
    ra = lax.broadcasted_iota(jnp.int32, (CHUNK, CHUNK), 0) // 64
    ca = lax.broadcasted_iota(jnp.int32, (CHUNK, CHUNK), 1) // 64
    same_head = (ra == ca).astype(F32).astype(BF16)
    rm = lax.broadcasted_iota(jnp.int32, (rows, rows), 0) % PG
    cm = lax.broadcasted_iota(jnp.int32, (rows, rows), 1) % PG
    mask[...] = (rm == cm).astype(F32).astype(BF16)

    def query_copy(k):
        return remote(qall.at[me_d], qall.at[me_d], qs_sem.at[k - 1], qr_sem.at[k - 1], "dp", ahead("dp", k))

    def meta_copy(k):
        return remote(meta.at[me_d], meta.at[me_d], ms_sem.at[k - 1], mr_sem.at[k - 1], "dp", ahead("dp", k))

    lead = max(1, groups // 2)
    order = range(1, ns)

    def rows_copy(f, k):
        peer = ahead("seq", k)
        return remote(
            obuf.at[f, pl.ds(peer * groups, lead)], recv.at[pl.ds(0, lead), me_s, f],
            as_sem.at[f, k - 1], ar_sem.at[f, k - 1], "seq", peer,
        )

    def group_copy(g, k):
        peer = ahead("seq", k)
        return remote(
            obuf.at[:, peer * groups + g], recv.at[g, me_s],
            bs_sem.at[g - lead, k - 1], br_sem.at[g - lead, k - 1], "seq", peer,
        )

    def spatial(f, first_time):
        frame_load(f).wait()
        normed = layer_norm(vbuf[f].astype(F32))
        for c in range(chunks):
            at = CHUNK * c
            if first_time:
                for third in range(3):
                    loads[3 * c + third].wait()
            q = dot(normed, sq[:, at:at + CHUNK])
            k = dot(normed, sq[:, width + at:width + at + CHUNK])
            v = dot(normed, sq[:, 2 * width + at:2 * width + at + CHUNK]).astype(BF16)
            qn = head_unit(q, same_head, SHARP).astype(BF16)
            kn = head_unit(k, same_head, 1.0).astype(BF16)
            bl[:, at:at + CHUNK] = blend(qn, kn, v, low, high, None)

    def spatial_out(f):
        for c in range(chunks):
            at = CHUNK * c
            update = dot(bl[...], so[:, at:at + CHUNK])
            obuf[f, :, :, at:at + CHUNK] = (
                vbuf[f, :, at:at + CHUNK].astype(F32) + update
            ).astype(BF16).reshape(patches // PG, PG, CHUNK)
        for k in order:
            rows_copy(f, k).start()

    spatial(0, True)
    loads[first].wait()
    pl.semaphore_wait(barrier, nd * ns - 1)
    spatial_out(0)
    for load in query_loads:
        load.wait()
    for k in range(1, nd):
        query_copy(k).start()
    per = 128 // lq
    tile = []
    for source in (qlen, qpos):
        for r in range(mrows):
            row = jnp.zeros((1, 128), jnp.int32)
            for c in range(per):
                row = jnp.where(lane128 // lq == c, source[r * per + c], row)
            tile.append(row)
    tile.append(jnp.zeros((8 - 2 * mrows, 128), jnp.int32))
    meta[me_d] = jnp.concatenate(tile, axis=0)
    for k in range(1, nd):
        meta_copy(k).start()

    @pl.loop(1, frames)
    def _(f):
        spatial(f, False)
        spatial_out(f)

    for g in range(lead, groups):
        for k in order:
            group_copy(g, k).start()
    for g in range(groups):
        recv[g, me_s] = obuf[:, me_s * groups + g]

    for k in range(1, nd):
        query_copy(k).wait()
        meta_copy(k).wait()
    for d in range(nd):
        qf = qall[d].astype(F32).T
        norm = lax.rsqrt(jnp.sum(qf * qf, axis=0, keepdims=True) + 1e-06)
        qht[:, d * qb:(d + 1) * qb] = (qf * norm).astype(BF16)
    sums[...] = jnp.zeros_like(sums)
    qs[...] = jnp.zeros_like(qs)
    for i in range(first + 1, first + 4):
        loads[i].wait()
    for f in range(frames):
        for k in order:
            rows_copy(f, k).wait_recv()

    @pl.loop(0, groups)
    def _(g):
        @pl.when(g >= lead)
        def _():
            for k in order:
                group_copy(g, k).wait_recv()

        x = recv[g].astype(F32).reshape(rows, width)
        normed = layer_norm(x)
        for c in range(chunks):
            at = CHUNK * c
            q = dot(normed, tq[:, at:at + CHUNK])
            k = dot(normed, tq[:, width + at:width + at + CHUNK])
            v = dot(normed, tq[:, 2 * width + at:2 * width + at + CHUNK]).astype(BF16)
            qn = head_unit(q, same_head, SHARP).astype(BF16)
            kn = head_unit(k, same_head, 1.0).astype(BF16)
            bl2[:, at:at + CHUNK] = blend(qn, kn, v, low, high, mask[...])
        mixed = x + dot(bl2[...], to[...])
        normed = layer_norm(mixed.astype(BF16).astype(F32))
        proj = dot(normed, pw[...])
        key = (proj * lax.rsqrt(jnp.sum(proj * proj, axis=-1, keepdims=True) + 1e-06)).astype(BF16)
        kh[g] = key
        for c in range(qt // CHUNK):
            cols = slice(CHUNK * c, CHUNK * c + CHUNK)
            e = jnp.exp((dot(key, qht[:, cols]) - 1.0) * (1.0 / TEMPER))
            sums[:, cols] += jnp.sum(e, axis=0, keepdims=True)
            eb = e.astype(BF16)
            ebuf[g, :, cols] = eb
            qs[:, cols] += dot_tn(key, eb)

    for d in range(nd):
        for r in range(mrows):
            at = d * qb + 128 * r
            srecv[me_s, d, r:r + 1, :] = sums[:, at:at + 128]

    def sums_copy(k):
        return remote(srecv.at[me_s], srecv.at[me_s], ss_sem.at[k - 1], sr_sem.at[k - 1], "seq", ahead("seq", k))

    def block_sums_copy(k, c):
        i = (k - 1) * ns + c
        peer_d = ahead("dp", k)
        return pltpu.make_async_remote_copy(
            src_ref=srecv.at[me_s, peer_d], dst_ref=xrecv.at[me_d, me_s],
            send_sem=xs_sem.at[i], recv_sem=xr_sem.at[i],
            device_id={"dp": peer_d, "seq": ahead("seq", c)}, device_id_type=pl.DeviceIdType.MESH,
        )

    for k in range(ns - 1, 0, -1):
        sums_copy(k).start()
    for k in range(nd - 1, 0, -1):
        for c in range(ns - 1, -1, -1):
            block_sums_copy(k, c).start()

    for d in range(nd):
        part[d] = qs[:, d * qb:(d + 1) * qb].T.astype(BF16).reshape(2, qb // 2, 128)
    me_c = me_s % 2
    me_z = me_s // 2
    prec[me_d, me_c] = part[me_d, me_c]
    near = [(k, c) for k in range(nd) for c in range(2) if k + c > 0]

    def part_copy(i):
        k, c = near[i]
        peer_d = ahead("dp", k)
        peer_s = ahead("seq", c)
        return pltpu.make_async_remote_copy(
            src_ref=part.at[peer_d, peer_s % 2], dst_ref=prec.at[me_d, me_c],
            send_sem=ps_sem.at[i], recv_sem=pr_sem.at[i],
            device_id={"dp": peer_d, "seq": peer_s}, device_id_type=pl.DeviceIdType.MESH,
        )

    for i in range(len(near)):
        part_copy(i).start()

    seg_a = lax.broadcasted_iota(jnp.int32, (128, 128), 0) // lq
    seg_b = lax.broadcasted_iota(jnp.int32, (128, 128), 1) // lq
    seg = (seg_a == seg_b).astype(F32)
    slot = lax.broadcasted_iota(jnp.int32, (1, 128), 1) % lq

    def pair_terms(total, lens, hit):
        valid = (slot < lens).astype(F32)
        count = lens.astype(F32)
        smooth = (1.0 + TEMPER * jnp.log(total)) * valid
        score = jnp.dot(smooth, seg, precision=lax.Precision.HIGHEST, preferred_element_type=F32) / count
        sign = jnp.where(hit, 1.0, -1.0)
        margin = sign * (SLOPE * score + OFFSET)
        coeff = -sign * SLOPE / (1.0 + jnp.exp(margin)) * valid / count
        return margin, coeff / total

    for k in range(1, ns):
        sums_copy(k).wait()
    for k in range(1, nd):
        for c in range(ns):
            block_sums_copy(k, c).wait()
    for s in range(ns):
        xrecv[me_d, s] = srecv[s, me_d]
    block_total = []
    for d in range(nd):
        total = xrecv[d, 0]
        for s in range(1, ns):
            total = total + xrecv[d, s]
        block_total.append(total)
    block_total = jnp.concatenate(block_total, axis=0)
    block_len = jnp.concatenate([meta[me_d, :mrows]] * nd, axis=0)
    block_pos = jnp.concatenate([meta[me_d, mrows:2 * mrows]] * nd, axis=0)
    block_video = lax.broadcasted_iota(jnp.int32, (nd * mrows, 128), 0) // mrows
    _, block_scale = pair_terms(block_total, block_len, block_pos == block_video)
    half = mrows // 2
    tall = block_scale.T
    for i in range(len(near)):
        part_copy(i).wait()
    pieces = []
    for h in range(half):
        acc = jnp.zeros((128, 128), F32)
        for d in range(nd):
            at = d * mrows + h
            weight = jnp.where(me_c == 0, tall[:, at:at + 1], tall[:, at + half:at + half + 1])
            both = prec[d, 0, 128 * h:128 * h + 128].astype(F32) + prec[d, 1, 128 * h:128 * h + 128].astype(F32)
            acc = acc + both * weight
        pieces.append(acc.astype(BF16))
    zrec[me_z] = jnp.concatenate(pieces, axis=0)

    def chip_copy(k):
        return remote(zrec.at[me_z], zrec.at[me_z], rs_sem.at[k - 1], rr_sem.at[k - 1], "seq", ahead("seq", 2 * k))

    for k in range(ns // 2 - 1, 0, -1):
        chip_copy(k).start()

    trows = qt // 128
    total = []
    for d in range(nd):
        rows_d = srecv[0, d]
        for s in range(1, ns):
            rows_d = rows_d + srecv[s, d]
        total.append(rows_d)
    total = jnp.concatenate(total, axis=0)
    all_len = jnp.concatenate([meta[d, :mrows] for d in range(nd)], axis=0)
    all_pos = jnp.concatenate([meta[d, mrows:2 * mrows] for d in range(nd)], axis=0)
    margin, scale = pair_terms(total, all_len, all_pos == me_d)
    wrow = jnp.concatenate([scale[r:r + 1] for r in range(trows)], axis=1)
    wq = (qht[...].astype(F32) * wrow).astype(BF16)

    def grad_out(b):
        cols = pl.ds(16 * b, 16)
        return pltpu.make_async_copy(vgbuf.at[0, :, cols, :], vg.at[0, :, cols, :], v_sem.at[b])

    for b in range(ploc // 16):
        halves = [
            (dot_nt(ebuf[2 * b + h], wq) * float(fall * patches)).reshape(fall, PG, 128)
            for h in range(2)
        ]
        vgbuf[0, :, 16 * b:16 * b + 16, :] = jnp.concatenate(halves, axis=1).astype(BF16)
        grad_out(b).start()

    tail = jnp.exp(-jnp.abs(margin))
    losses = jnp.maximum(-margin, 0.0) + jnp.log1p(tail)
    nq = qt // lq
    lr = lax.broadcasted_iota(jnp.int32, (128, nq), 0)
    lc = lax.broadcasted_iota(jnp.int32, (128, nq), 1)
    pick = (lr == lc % per * lq).astype(F32)
    spread = jnp.dot(losses, pick, precision=lax.Precision.HIGHEST, preferred_element_type=F32)
    qr = lax.broadcasted_iota(jnp.int32, (trows, nq), 0)
    qc = lax.broadcasted_iota(jnp.int32, (trows, nq), 1) // per
    loss[...] = jnp.sum(jnp.where(qr == qc, spread, 0.0), axis=0, keepdims=True)

    for k in range(1, ns // 2):
        chip_copy(k).wait()
    acc = zrec[0].astype(F32)
    for z in range(1, ns // 2):
        acc = acc + zrec[z].astype(F32)
    gath[me_c] = (acc * float(lq)).astype(BF16)
    swap = remote(gath.at[me_c], gath.at[me_c], gs_sem.at[0], gr_sem.at[0], "seq", ahead("seq", 1))
    swap.start()
    swap.wait()
    qg[...] = gath[...].reshape(qg.shape)
    for b in range(ploc // 16):
        grad_out(b).wait()

    @pl.loop(0, frames)
    def _(f):
        for k in range(1, ns):
            rows_copy(f, k).wait_send()

    for g in range(lead, groups):
        for k in order:
            group_copy(g, k).wait_send()


def finish(vg_in, qg_in, loss_in, vg_out, qg_out, loss_out, vg_buf, qg_buf, loss_buf, in_sem, out_sem):
    steps = ((vg_in, vg_buf, vg_out), (qg_in, qg_buf, qg_out), (loss_in, loss_buf, loss_out))
    fetch = [pltpu.make_async_copy(a, b, in_sem.at[i]) for i, (a, b, _) in enumerate(steps)]
    store = [pltpu.make_async_copy(b, c, out_sem.at[i]) for i, (_, b, c) in enumerate(steps)]
    for copy in fetch:
        copy.start()
    for i in range(len(steps)):
        fetch[i].wait()
        store[i].start()
    for copy in store:
        copy.wait()


def body(nd, ns, video, space_qkv, space_out, time_qkv, time_out, proj_weight, queries, query_len, positive):
    videos_dev, frames, patches, width = video.shape
    assert videos_dev == 1
    qdev, lq, embed = queries.shape
    ploc = patches // ns
    fall = frames * ns
    rows = fall * PG
    groups = ploc // PG
    qb = qdev * lq
    qt = nd * qb
    vmem = pltpu.VMEM
    dma = pltpu.SemaphoreType.DMA
    anyspec = pl.BlockSpec(memory_space=pl.ANY)
    vspec = pl.BlockSpec(memory_space=pltpu.VMEM)
    vg, qg, loss = pl.pallas_call(
        functools.partial(kernel, nd, ns, lq),
        out_shape=(
            jax.ShapeDtypeStruct((1, fall, ploc, embed), BF16),
            jax.ShapeDtypeStruct((qdev, lq, embed), BF16),
            jax.ShapeDtypeStruct((1, nd * qdev), F32),
        ),
        in_specs=[anyspec] * 9,
        out_specs=(anyspec, vspec, vspec),
        scratch_shapes=[
            vmem((frames, patches, width), BF16),
            vmem(space_qkv.shape, BF16),
            vmem(space_out.shape, BF16),
            vmem(time_qkv.shape, BF16),
            vmem(time_out.shape, BF16),
            vmem(proj_weight.shape, BF16),
            vmem((frames, patches // PG, PG, width), BF16),
            vmem((patches, width), BF16),
            vmem((groups, ns, frames, PG, width), BF16),
            vmem((rows, width), BF16),
            vmem((rows, rows), BF16),
            vmem((groups, rows, embed), BF16),
            vmem((groups, rows, qt), BF16),
            vmem((1, qt), F32),
            vmem((embed, qt), F32),
            vmem((nd, qb, embed), BF16),
            vmem((nd, 8, 128), jnp.int32),
            vmem((ns, nd, qb // 128, 128), F32),
            vmem((nd, ns, qb // 128, 128), F32),
            vmem((nd, 2, qb // 2, embed), BF16),
            vmem((nd, 2, qb // 2, embed), BF16),
            vmem((ns // 2, qb // 2, embed), BF16),
            vmem((2, qb // 2, embed), BF16),
            vmem((embed, qt), BF16),
            vmem((1, fall, ploc, embed), BF16),
            pltpu.SMEM((qdev,), jnp.int32),
            pltpu.SMEM((qdev,), jnp.int32),
            dma((frames,)), dma((3 * (width // CHUNK) + 4,)),
            dma((3,)), dma((ploc // 16,)),
            dma((frames, ns - 1)), dma((frames, ns - 1)),
            dma((max(1, groups - groups // 2), ns - 1)), dma((max(1, groups - groups // 2), ns - 1)),
            dma((nd - 1,)), dma((nd - 1,)),
            dma((nd - 1,)), dma((nd - 1,)),
            dma((ns - 1,)), dma((ns - 1,)),
            dma(((nd - 1) * ns,)), dma(((nd - 1) * ns,)),
            dma((2 * nd - 1,)), dma((2 * nd - 1,)),
            dma((ns // 2 - 1,)), dma((ns // 2 - 1,)),
            dma((1,)), dma((1,)),
        ],
        compiler_params=pltpu.CompilerParams(
            collective_id=0, has_side_effects=True, vmem_limit_bytes=60 * 1024 * 1024
        ),
    )(
        video, space_qkv, space_out, time_qkv, time_out, proj_weight,
        queries.reshape(qb, embed), query_len, positive,
    )
    vg, qg, loss = pl.pallas_call(
        finish,
        out_shape=(
            jax.ShapeDtypeStruct(vg.shape, BF16),
            jax.ShapeDtypeStruct(qg.shape, BF16),
            jax.ShapeDtypeStruct(loss.shape, F32),
        ),
        in_specs=[anyspec] * 3,
        out_specs=(anyspec, anyspec, anyspec),
        scratch_shapes=[
            vmem(vg.shape, BF16), vmem(qg.shape, BF16), vmem(loss.shape, F32), dma((3,)), dma((3,)),
        ],
    )(vg, qg, loss)
    return vg, qg, loss.reshape(nd * qdev, 1)


def solution(mesh):
    nd, ns = mesh.shape["dp"], mesh.shape["seq"]
    placed = (
        P("dp", "seq", None, None),
        P(), P(), P(), P(), P(),
        P("dp", None, None),
        P("dp"),
        P("dp"),
    )
    return jax.shard_map(
        functools.partial(body, nd, ns),
        mesh=mesh,
        in_specs=placed,
        out_specs=(P("dp", None, "seq", None), P("dp", None, None), P(None, "dp")),
        check_vma=False,
    )
```

```python
import functools

import jax
import jax.numpy as jnp
from jax import lax
from jax.experimental import pallas as pl
from jax.experimental.pallas import tpu as pltpu
from jax.sharding import PartitionSpec as P

HEADS = 12
TEMPER = 0.05
SLOPE = 10.0
OFFSET = -5.0
SHARP = 10.0
LOG2E = 1.4426950408889634
CHUNK = 256
PG = 8
F32 = jnp.float32
BF16 = jnp.bfloat16


def dot(a, b):
    return jnp.dot(a, b, preferred_element_type=F32)


def dot_nt(a, b):
    return lax.dot_general(a, b, (((1,), (1,)), ((), ())), preferred_element_type=F32)


def dot_tn(a, b):
    return lax.dot_general(a, b, (((0,), (0,)), ((), ())), preferred_element_type=F32)


def layer_norm(values):
    center = values - jnp.mean(values, axis=-1, keepdims=True)
    spread = jnp.mean(center * center, axis=-1, keepdims=True)
    return (center * lax.rsqrt(spread + 1e-05)).astype(BF16)


def head_unit(values, same_head, scale):
    total = dot((values * values).astype(BF16), same_head)
    return values * (lax.rsqrt(total + 1e-06) * scale)


def scores(qn, kn, low, high, mask):
    out = []
    for p in range(CHUNK // 128):
        cols = slice(128 * p, 128 * p + 128)
        for half in (low, high):
            e = jnp.exp2(dot_nt(qn[:, cols] * half, kn[:, cols])).astype(BF16)
            if mask is not None:
                e = e * mask
            out.append(e)
    return out


def mix(weights, v):
    rows = v.shape[0]
    lane = lax.broadcasted_iota(jnp.int32, (rows, 128), 1) < 64
    ones = jnp.ones((rows, 128), BF16)
    out = []
    for p in range(CHUNK // 128):
        vx = jnp.concatenate([v[:, 128 * p:128 * p + 128], ones], axis=1)
        res = [dot(weights[2 * p + h], vx) for h in range(2)]
        num = jnp.where(lane, res[0][:, :128], res[1][:, :128])
        den = jnp.where(lane, res[0][:, 128:], res[1][:, 128:])
        out.append((num / den).astype(BF16))
    return jnp.concatenate(out, axis=1)


def attend(normed, w, same_head, low, high, mask, ready, put):
    width = normed.shape[1]
    chunks = width // CHUNK

    def project(c):
        ready(c)
        at = CHUNK * c
        q = dot(normed, w[:, at:at + CHUNK])
        k = dot(normed, w[:, width + at:width + at + CHUNK])
        v = dot(normed, w[:, 2 * width + at:2 * width + at + CHUNK]).astype(BF16)
        return q, k, v

    def unit(q, k):
        qn = head_unit(q, same_head, SHARP * LOG2E).astype(BF16)
        return qn, head_unit(k, same_head, 1.0).astype(BF16)

    q, k, v = project(0)
    qn, kn = unit(q, k)
    for c in range(chunks):
        now = v
        if c + 1 < chunks:
            q, k, v = project(c + 1)
        weights = scores(qn, kn, low, high, mask)
        if c + 1 < chunks:
            qn, kn = unit(q, k)
        put(c, mix(weights, now))


def kernel(
    nd, ns, lq,
    video, w_sq, w_so, w_tq, w_to, w_p, queries, qlen_in, qpos_in,
    vg, qg, loss,
    vbuf, sq, so, tq, to, pw, obuf, bl, recv, bl2, mask, kh, ebuf, sums, qs,
    qall, meta, srecv, xrecv, part, prec, zrec, gath, qht, vgbuf, qlen, qpos,
    in_sem, w_sem, q_sem, v_sem, as_sem, ar_sem, bs_sem, br_sem, qs_sem, qr_sem, ms_sem, mr_sem, ss_sem, sr_sem,
    xs_sem, xr_sem, ps_sem, pr_sem, rs_sem, rr_sem, gs_sem, gr_sem,
):
    frames, patches, width = vbuf.shape
    ploc = patches // ns
    fall = frames * ns
    rows = fall * PG
    groups = ploc // PG
    chunks = width // CHUNK
    qb = qall.shape[1]
    qt = nd * qb
    mrows = qb // 128
    me_d = lax.axis_index("dp")
    me_s = lax.axis_index("seq")

    def ahead(axis, k):
        if axis == "dp":
            return lax.rem(me_d + k, nd)
        peer, bit = 0, 1
        while bit < ns:
            digit = (me_s // bit) % 2
            peer = peer + bit * (1 - digit if k & bit else digit)
            bit *= 2
        return peer

    def remote(src, dst, send, recv_at, axis, peer):
        return pltpu.make_async_remote_copy(
            src_ref=src, dst_ref=dst, send_sem=send, recv_sem=recv_at,
            device_id={axis: peer}, device_id_type=pl.DeviceIdType.MESH,
        )

    pairs = []
    for c in range(chunks):
        for third in range(3):
            cols = pl.ds(third * width + CHUNK * c, CHUNK)
            pairs.append((w_sq.at[:, cols], sq.at[:, cols]))
    first = len(pairs)
    pairs += [(w_so, so), (w_tq, tq), (w_to, to), (w_p, pw)]
    loads = [
        pltpu.make_async_copy(src, dst, w_sem.at[i]) for i, (src, dst) in enumerate(pairs)
    ]

    def frame_load(f):
        return pltpu.make_async_copy(video.at[0, f], vbuf.at[f], in_sem.at[f])

    query_loads = [
        pltpu.make_async_copy(queries, qall.at[me_d], q_sem.at[0]),
        pltpu.make_async_copy(qlen_in, qlen, q_sem.at[1]),
        pltpu.make_async_copy(qpos_in, qpos, q_sem.at[2]),
    ]
    frame_load(0).start()
    for i in range(first + 1):
        loads[i].start()
    for load in query_loads:
        load.start()
    for f in range(1, frames):
        frame_load(f).start()
    for i in range(first + 1, first + 4):
        loads[i].start()

    barrier = pltpu.get_barrier_semaphore()
    others = [(k, c) for k in range(nd) for c in range(ns) if k + c > 0]
    for k, c in others:
        pl.semaphore_signal(
            barrier, inc=1, device_id={"dp": ahead("dp", k), "seq": ahead("seq", c)},
            device_id_type=pl.DeviceIdType.MESH,
        )

    lane128 = lax.broadcasted_iota(jnp.int32, (1, 128), 1)
    low = (lane128 < 64).astype(F32).astype(BF16)
    high = (lane128 >= 64).astype(F32).astype(BF16)
    ra = lax.broadcasted_iota(jnp.int32, (CHUNK, CHUNK), 0) // 64
    ca = lax.broadcasted_iota(jnp.int32, (CHUNK, CHUNK), 1) // 64
    same_head = (ra == ca).astype(F32).astype(BF16)
    rm = lax.broadcasted_iota(jnp.int32, (rows, rows), 0) % PG
    cm = lax.broadcasted_iota(jnp.int32, (rows, rows), 1) % PG
    mask[...] = (rm == cm).astype(F32).astype(BF16)

    def query_copy(k):
        return remote(qall.at[me_d], qall.at[me_d], qs_sem.at[k - 1], qr_sem.at[k - 1], "dp", ahead("dp", k))

    def meta_copy(k):
        return remote(meta.at[me_d], meta.at[me_d], ms_sem.at[k - 1], mr_sem.at[k - 1], "dp", ahead("dp", k))

    lead = max(1, groups // 2)
    order = range(1, ns)

    def rows_copy(f, k):
        peer = ahead("seq", k)
        return remote(
            obuf.at[f, pl.ds(peer * groups, lead)], recv.at[pl.ds(0, lead), me_s, f],
            as_sem.at[f, k - 1], ar_sem.at[f, k - 1], "seq", peer,
        )

    def group_copy(g, k):
        peer = ahead("seq", k)
        return remote(
            obuf.at[:, peer * groups + g], recv.at[g, me_s],
            bs_sem.at[g - lead, k - 1], br_sem.at[g - lead, k - 1], "seq", peer,
        )

    def spatial(f, first_time):
        frame_load(f).wait()
        normed = layer_norm(vbuf[f].astype(F32))

        def ready(c):
            if first_time:
                for third in range(3):
                    loads[3 * c + third].wait()

        def put(c, value):
            bl[:, CHUNK * c:CHUNK * c + CHUNK] = value

        attend(normed, sq, same_head, low, high, None, ready, put)

    def spatial_out(f):
        for c in range(chunks):
            at = CHUNK * c
            update = dot(bl[...], so[:, at:at + CHUNK])
            obuf[f, :, :, at:at + CHUNK] = (
                vbuf[f, :, at:at + CHUNK].astype(F32) + update
            ).astype(BF16).reshape(patches // PG, PG, CHUNK)
        for k in reversed(order):
            rows_copy(f, k).start()

    spatial(0, True)
    loads[first].wait()
    pl.semaphore_wait(barrier, nd * ns - 1)
    spatial_out(0)
    for load in query_loads:
        load.wait()
    for k in range(1, nd):
        query_copy(k).start()
    per = 128 // lq
    tile = []
    for source in (qlen, qpos):
        for r in range(mrows):
            row = jnp.zeros((1, 128), jnp.int32)
            for c in range(per):
                row = jnp.where(lane128 // lq == c, source[r * per + c], row)
            tile.append(row)
    tile.append(jnp.zeros((8 - 2 * mrows, 128), jnp.int32))
    meta[me_d] = jnp.concatenate(tile, axis=0)
    for k in range(1, nd):
        meta_copy(k).start()

    @pl.loop(1, frames)
    def _(f):
        spatial(f, False)
        spatial_out(f)

    line = me_s // (ns // 4)
    inner = (line == 1) | (line == 2)
    late = [k for k in order if k >= ns // 2]
    soon = [k for k in order if not (k >= ns // 2)]
    for g in range(lead, groups):
        for k in soon:
            group_copy(g, k).start()

    @pl.when(jnp.logical_not(inner))
    def _():
        for g in range(lead, groups):
            for k in late:
                group_copy(g, k).start()

    for g in range(groups):
        recv[g, me_s] = obuf[:, me_s * groups + g]

    for k in range(1, nd):
        query_copy(k).wait()
        meta_copy(k).wait()
    for d in range(nd):
        qf = qall[d].astype(F32).T
        norm = lax.rsqrt(jnp.sum(qf * qf, axis=0, keepdims=True) + 1e-06)
        qht[:, d * qb:(d + 1) * qb] = (qf * norm).astype(BF16)
    sums[...] = jnp.zeros_like(sums)
    qs[...] = jnp.zeros_like(qs)
    for i in range(first + 1, first + 4):
        loads[i].wait()
    for f in range(frames):
        for k in order:
            rows_copy(f, k).wait_recv()

    @pl.loop(0, groups)
    def _(g):
        @pl.when(jnp.logical_and(inner, jnp.logical_and(g >= 0, g + lead < groups)))
        def _():
            for k in late:
                group_copy(g + lead, k).start()

        @pl.when(g >= lead)
        def _():
            for k in order:
                group_copy(g, k).wait_recv()

        x = recv[g].astype(F32).reshape(rows, width)
        normed = layer_norm(x)

        def put(c, value):
            bl2[:, CHUNK * c:CHUNK * c + CHUNK] = value

        attend(normed, tq, same_head, low, high, mask[...], lambda c: None, put)
        mixed = x + dot(bl2[...], to[...])
        normed = layer_norm(mixed.astype(BF16).astype(F32))
        proj = dot(normed, pw[...])
        key = (proj * lax.rsqrt(jnp.sum(proj * proj, axis=-1, keepdims=True) + 1e-06)).astype(BF16)
        kh[g] = key

        def similar(c):
            cols = slice(CHUNK * c, CHUNK * c + CHUNK)
            e = jnp.exp2(dot(key, qht[:, cols]) * (LOG2E / TEMPER) - LOG2E / TEMPER)
            sums[:, cols] += jnp.sum(e, axis=0, keepdims=True)
            eb = e.astype(BF16)
            ebuf[g, :, cols] = eb
            return eb

        eb = similar(0)
        for c in range(qt // CHUNK):
            later = similar(c + 1) if c + 1 < qt // CHUNK else None
            qs[:, CHUNK * c:CHUNK * c + CHUNK] += dot_tn(key, eb)
            eb = later

    for d in range(nd):
        for r in range(mrows):
            at = d * qb + 128 * r
            srecv[me_s, d, r:r + 1, :] = sums[:, at:at + 128]

    def sums_copy(k):
        return remote(srecv.at[me_s], srecv.at[me_s], ss_sem.at[k - 1], sr_sem.at[k - 1], "seq", ahead("seq", k))

    def block_sums_copy(k, c):
        i = (k - 1) * ns + c
        peer_d = ahead("dp", k)
        return pltpu.make_async_remote_copy(
            src_ref=srecv.at[me_s, peer_d], dst_ref=xrecv.at[me_d, me_s],
            send_sem=xs_sem.at[i], recv_sem=xr_sem.at[i],
            device_id={"dp": peer_d, "seq": ahead("seq", c)}, device_id_type=pl.DeviceIdType.MESH,
        )

    for k in range(ns - 1, 0, -1):
        sums_copy(k).start()
    for k in range(nd - 1, 0, -1):
        for c in range(ns - 1, -1, -1):
            block_sums_copy(k, c).start()

    for d in range(nd):
        part[d] = qs[:, d * qb:(d + 1) * qb].T.astype(BF16).reshape(2, qb // 2, 128)
    me_c = me_s % 2
    me_z = me_s // 2
    prec[me_d, me_c] = part[me_d, me_c]
    near = [(k, c) for k in range(nd) for c in range(2) if k + c > 0]

    def part_copy(i):
        k, c = near[i]
        peer_d = ahead("dp", k)
        peer_s = ahead("seq", c)
        return pltpu.make_async_remote_copy(
            src_ref=part.at[peer_d, peer_s % 2], dst_ref=prec.at[me_d, me_c],
            send_sem=ps_sem.at[i], recv_sem=pr_sem.at[i],
            device_id={"dp": peer_d, "seq": peer_s}, device_id_type=pl.DeviceIdType.MESH,
        )

    for i in range(len(near)):
        part_copy(i).start()

    seg_a = lax.broadcasted_iota(jnp.int32, (128, 128), 0) // lq
    seg_b = lax.broadcasted_iota(jnp.int32, (128, 128), 1) // lq
    seg = (seg_a == seg_b).astype(F32)
    slot = lax.broadcasted_iota(jnp.int32, (1, 128), 1) % lq

    def pair_terms(total, lens, hit):
        valid = (slot < lens).astype(F32)
        count = lens.astype(F32)
        smooth = (1.0 + TEMPER * jnp.log(total)) * valid
        score = jnp.dot(smooth, seg, precision=lax.Precision.HIGHEST, preferred_element_type=F32) / count
        sign = jnp.where(hit, 1.0, -1.0)
        margin = sign * (SLOPE * score + OFFSET)
        coeff = -sign * SLOPE / (1.0 + jnp.exp(margin)) * valid / count
        return margin, coeff / total

    for k in range(1, ns):
        sums_copy(k).wait()
    for k in range(1, nd):
        for c in range(ns):
            block_sums_copy(k, c).wait()
    for s in range(ns):
        xrecv[me_d, s] = srecv[s, me_d]
    block_total = []
    for d in range(nd):
        total = xrecv[d, 0]
        for s in range(1, ns):
            total = total + xrecv[d, s]
        block_total.append(total)
    block_total = jnp.concatenate(block_total, axis=0)
    block_len = jnp.concatenate([meta[me_d, :mrows]] * nd, axis=0)
    block_pos = jnp.concatenate([meta[me_d, mrows:2 * mrows]] * nd, axis=0)
    block_video = lax.broadcasted_iota(jnp.int32, (nd * mrows, 128), 0) // mrows
    _, block_scale = pair_terms(block_total, block_len, block_pos == block_video)
    half = mrows // 2
    tall = block_scale.T
    for i in range(len(near)):
        part_copy(i).wait()
    pieces = []
    for h in range(half):
        acc = jnp.zeros((128, 128), F32)
        for d in range(nd):
            at = d * mrows + h
            weight = jnp.where(me_c == 0, tall[:, at:at + 1], tall[:, at + half:at + half + 1])
            both = prec[d, 0, 128 * h:128 * h + 128].astype(F32) + prec[d, 1, 128 * h:128 * h + 128].astype(F32)
            acc = acc + both * weight
        pieces.append(acc.astype(BF16))
    zrec[me_z] = jnp.concatenate(pieces, axis=0)

    def chip_copy(k):
        return remote(zrec.at[me_z], zrec.at[me_z], rs_sem.at[k - 1], rr_sem.at[k - 1], "seq", ahead("seq", 2 * k))

    for k in range(ns // 2 - 1, 0, -1):
        chip_copy(k).start()

    trows = qt // 128
    total = []
    for d in range(nd):
        rows_d = srecv[0, d]
        for s in range(1, ns):
            rows_d = rows_d + srecv[s, d]
        total.append(rows_d)
    total = jnp.concatenate(total, axis=0)
    all_len = jnp.concatenate([meta[d, :mrows] for d in range(nd)], axis=0)
    all_pos = jnp.concatenate([meta[d, mrows:2 * mrows] for d in range(nd)], axis=0)
    margin, scale = pair_terms(total, all_len, all_pos == me_d)
    wrow = jnp.concatenate([scale[r:r + 1] for r in range(trows)], axis=1)
    wq = (qht[...].astype(F32) * wrow).astype(BF16)

    def grad_out(b):
        cols = pl.ds(16 * b, 16)
        return pltpu.make_async_copy(vgbuf.at[0, :, cols, :], vg.at[0, :, cols, :], v_sem.at[b])

    for b in range(ploc // 16):
        halves = [
            (dot_nt(ebuf[2 * b + h], wq) * float(fall * patches)).reshape(fall, PG, 128)
            for h in range(2)
        ]
        vgbuf[0, :, 16 * b:16 * b + 16, :] = jnp.concatenate(halves, axis=1).astype(BF16)
        grad_out(b).start()

    tail = jnp.exp(-jnp.abs(margin))
    losses = jnp.maximum(-margin, 0.0) + jnp.log1p(tail)
    nq = qt // lq
    lr = lax.broadcasted_iota(jnp.int32, (128, nq), 0)
    lc = lax.broadcasted_iota(jnp.int32, (128, nq), 1)
    pick = (lr == lc % per * lq).astype(F32)
    spread = jnp.dot(losses, pick, precision=lax.Precision.HIGHEST, preferred_element_type=F32)
    qr = lax.broadcasted_iota(jnp.int32, (trows, nq), 0)
    qc = lax.broadcasted_iota(jnp.int32, (trows, nq), 1) // per
    loss[...] = jnp.sum(jnp.where(qr == qc, spread, 0.0), axis=0, keepdims=True)

    for k in range(1, ns // 2):
        chip_copy(k).wait()
    acc = zrec[0].astype(F32)
    for z in range(1, ns // 2):
        acc = acc + zrec[z].astype(F32)
    gath[me_c] = (acc * float(lq)).astype(BF16)
    swap = remote(gath.at[me_c], gath.at[me_c], gs_sem.at[0], gr_sem.at[0], "seq", ahead("seq", 1))
    swap.start()
    swap.wait()
    qg[...] = gath[...].reshape(qg.shape)
    for b in range(ploc // 16):
        grad_out(b).wait()

    @pl.loop(0, frames)
    def _(f):
        for k in range(1, ns):
            rows_copy(f, k).wait_send()

    for g in range(lead, groups):
        for k in order:
            group_copy(g, k).wait_send()


def finish(vg_in, qg_in, loss_in, vg_out, qg_out, loss_out, vg_buf, qg_buf, loss_buf, in_sem, out_sem):
    steps = ((vg_in, vg_buf, vg_out), (qg_in, qg_buf, qg_out), (loss_in, loss_buf, loss_out))
    fetch = [pltpu.make_async_copy(a, b, in_sem.at[i]) for i, (a, b, _) in enumerate(steps)]
    store = [pltpu.make_async_copy(b, c, out_sem.at[i]) for i, (_, b, c) in enumerate(steps)]
    for copy in fetch:
        copy.start()
    for i in range(len(steps)):
        fetch[i].wait()
        store[i].start()
    for copy in store:
        copy.wait()


def body(nd, ns, video, space_qkv, space_out, time_qkv, time_out, proj_weight, queries, query_len, positive):
    videos_dev, frames, patches, width = video.shape
    assert videos_dev == 1
    qdev, lq, embed = queries.shape
    ploc = patches // ns
    fall = frames * ns
    rows = fall * PG
    groups = ploc // PG
    qb = qdev * lq
    qt = nd * qb
    vmem = pltpu.VMEM
    dma = pltpu.SemaphoreType.DMA
    anyspec = pl.BlockSpec(memory_space=pl.ANY)
    vspec = pl.BlockSpec(memory_space=pltpu.VMEM)
    vg, qg, loss = pl.pallas_call(
        functools.partial(kernel, nd, ns, lq),
        out_shape=(
            jax.ShapeDtypeStruct((1, fall, ploc, embed), BF16),
            jax.ShapeDtypeStruct((qdev, lq, embed), BF16),
            jax.ShapeDtypeStruct((1, nd * qdev), F32),
        ),
        in_specs=[anyspec] * 9,
        out_specs=(anyspec, vspec, vspec),
        scratch_shapes=[
            vmem((frames, patches, width), BF16),
            vmem(space_qkv.shape, BF16),
            vmem(space_out.shape, BF16),
            vmem(time_qkv.shape, BF16),
            vmem(time_out.shape, BF16),
            vmem(proj_weight.shape, BF16),
            vmem((frames, patches // PG, PG, width), BF16),
            vmem((patches, width), BF16),
            vmem((groups, ns, frames, PG, width), BF16),
            vmem((rows, width), BF16),
            vmem((rows, rows), BF16),
            vmem((groups, rows, embed), BF16),
            vmem((groups, rows, qt), BF16),
            vmem((1, qt), F32),
            vmem((embed, qt), F32),
            vmem((nd, qb, embed), BF16),
            vmem((nd, 8, 128), jnp.int32),
            vmem((ns, nd, qb // 128, 128), F32),
            vmem((nd, ns, qb // 128, 128), F32),
            vmem((nd, 2, qb // 2, embed), BF16),
            vmem((nd, 2, qb // 2, embed), BF16),
            vmem((ns // 2, qb // 2, embed), BF16),
            vmem((2, qb // 2, embed), BF16),
            vmem((embed, qt), BF16),
            vmem((1, fall, ploc, embed), BF16),
            pltpu.SMEM((qdev,), jnp.int32),
            pltpu.SMEM((qdev,), jnp.int32),
            dma((frames,)), dma((3 * (width // CHUNK) + 4,)),
            dma((3,)), dma((ploc // 16,)),
            dma((frames, ns - 1)), dma((frames, ns - 1)),
            dma((max(1, groups - groups // 2), ns - 1)), dma((max(1, groups - groups // 2), ns - 1)),
            dma((nd - 1,)), dma((nd - 1,)),
            dma((nd - 1,)), dma((nd - 1,)),
            dma((ns - 1,)), dma((ns - 1,)),
            dma(((nd - 1) * ns,)), dma(((nd - 1) * ns,)),
            dma((2 * nd - 1,)), dma((2 * nd - 1,)),
            dma((ns // 2 - 1,)), dma((ns // 2 - 1,)),
            dma((1,)), dma((1,)),
        ],
        compiler_params=pltpu.CompilerParams(
            collective_id=0, has_side_effects=True, vmem_limit_bytes=60 * 1024 * 1024
        ),
    )(
        video, space_qkv, space_out, time_qkv, time_out, proj_weight,
        queries.reshape(qb, embed), query_len, positive,
    )
    vg, qg, loss = pl.pallas_call(
        finish,
        out_shape=(
            jax.ShapeDtypeStruct(vg.shape, BF16),
            jax.ShapeDtypeStruct(qg.shape, BF16),
            jax.ShapeDtypeStruct(loss.shape, F32),
        ),
        in_specs=[anyspec] * 3,
        out_specs=(anyspec, anyspec, anyspec),
        scratch_shapes=[
            vmem(vg.shape, BF16), vmem(qg.shape, BF16), vmem(loss.shape, F32), dma((3,)), dma((3,)),
        ],
    )(vg, qg, loss)
    return vg, qg, loss.reshape(nd * qdev, 1)


def solution(mesh):
    nd, ns = mesh.shape["dp"], mesh.shape["seq"]
    placed = (
        P("dp", "seq", None, None),
        P(), P(), P(), P(), P(),
        P("dp", None, None),
        P("dp"),
        P("dp"),
    )
    return jax.shard_map(
        functools.partial(body, nd, ns),
        mesh=mesh,
        in_specs=placed,
        out_specs=(P("dp", None, "seq", None), P("dp", None, None), P(None, "dp")),
        check_vma=False,
    )
```

```python
import functools

import jax
import jax.numpy as jnp
from jax import lax
from jax.experimental import pallas as pl
from jax.experimental.pallas import tpu as pltpu
from jax.sharding import PartitionSpec as P

HEADS = 12
TEMPER = 0.05
SLOPE = 10.0
OFFSET = -5.0
SHARP = 10.0
LOG2E = 1.4426950408889634
CHUNK = 256
PG = 8
F32 = jnp.float32
BF16 = jnp.bfloat16


def dot(a, b):
    return jnp.dot(a, b, preferred_element_type=F32)


def dot_nt(a, b):
    return lax.dot_general(a, b, (((1,), (1,)), ((), ())), preferred_element_type=F32)


def dot_tn(a, b):
    return lax.dot_general(a, b, (((0,), (0,)), ((), ())), preferred_element_type=F32)


def layer_norm(values):
    center = values - jnp.mean(values, axis=-1, keepdims=True)
    spread = jnp.mean(center * center, axis=-1, keepdims=True)
    return (center * lax.rsqrt(spread + 1e-05)).astype(BF16)


def head_unit(values, same_head, scale):
    total = dot((values * values).astype(BF16), same_head)
    return values * (lax.rsqrt(total + 1e-06) * scale)


def scores(qn, kn, low, high, mask):
    out = []
    for p in range(CHUNK // 128):
        cols = slice(128 * p, 128 * p + 128)
        for half in (low, high):
            e = jnp.exp2(dot_nt(qn[:, cols] * half, kn[:, cols])).astype(BF16)
            if mask is not None:
                e = e * mask
            out.append(e)
    return out


def mix(weights, v):
    rows = v.shape[0]
    lane = lax.broadcasted_iota(jnp.int32, (rows, 128), 1) < 64
    ones = jnp.ones((rows, 128), BF16)
    out = []
    for p in range(CHUNK // 128):
        vx = jnp.concatenate([v[:, 128 * p:128 * p + 128], ones], axis=1)
        res = [dot(weights[2 * p + h], vx) for h in range(2)]
        num = jnp.where(lane, res[0][:, :128], res[1][:, :128])
        den = jnp.where(lane, res[0][:, 128:], res[1][:, 128:])
        out.append((num / den).astype(BF16))
    return jnp.concatenate(out, axis=1)


def attend(normed, w, same_head, low, high, mask, ready, put):
    width = normed.shape[1]
    chunks = width // CHUNK

    def project(c):
        ready(c)
        at = CHUNK * c
        q = dot(normed, w[:, at:at + CHUNK])
        k = dot(normed, w[:, width + at:width + at + CHUNK])
        v = dot(normed, w[:, 2 * width + at:2 * width + at + CHUNK]).astype(BF16)
        return q, k, v

    def unit(q, k):
        qn = head_unit(q, same_head, SHARP * LOG2E).astype(BF16)
        return qn, head_unit(k, same_head, 1.0).astype(BF16)

    q, k, v = project(0)
    qn, kn = unit(q, k)
    for c in range(chunks):
        now = v
        if c + 1 < chunks:
            q, k, v = project(c + 1)
        weights = scores(qn, kn, low, high, mask)
        if c + 1 < chunks:
            qn, kn = unit(q, k)
        put(c, mix(weights, now))


def kernel(
    nd, ns, lq,
    video, w_sq, w_so, w_tq, w_to, w_p, queries, qlen_in, qpos_in,
    vg, qg, loss,
    vbuf, sq, so, tq, to, pw, obuf, bl, recv, bl2, mask, kh, ebuf, sums, qs,
    qall, meta, srecv, xrecv, part, prec, zrec, gath, qht, vgbuf, qlen, qpos,
    in_sem, w_sem, q_sem, v_sem, as_sem, ar_sem, bs_sem, br_sem, qs_sem, qr_sem, ms_sem, mr_sem, ss_sem, sr_sem,
    xs_sem, xr_sem, ps_sem, pr_sem, rs_sem, rr_sem, gs_sem, gr_sem,
):
    frames, patches, width = vbuf.shape
    ploc = patches // ns
    fall = frames * ns
    rows = fall * PG
    groups = ploc // PG
    chunks = width // CHUNK
    qb = qall.shape[1]
    qt = nd * qb
    mrows = qb // 128
    me_d = lax.axis_index("dp")
    me_s = lax.axis_index("seq")

    def ahead(axis, k):
        if axis == "dp":
            return lax.rem(me_d + k, nd)
        peer, bit = 0, 1
        while bit < ns:
            digit = (me_s // bit) % 2
            peer = peer + bit * (1 - digit if k & bit else digit)
            bit *= 2
        return peer

    def remote(src, dst, send, recv_at, axis, peer):
        return pltpu.make_async_remote_copy(
            src_ref=src, dst_ref=dst, send_sem=send, recv_sem=recv_at,
            device_id={axis: peer}, device_id_type=pl.DeviceIdType.MESH,
        )

    pairs = []
    for c in range(chunks):
        for third in range(3):
            cols = pl.ds(third * width + CHUNK * c, CHUNK)
            pairs.append((w_sq.at[:, cols], sq.at[:, cols]))
    first = len(pairs)
    pairs += [(w_so, so), (w_tq, tq), (w_to, to), (w_p, pw)]
    loads = [
        pltpu.make_async_copy(src, dst, w_sem.at[i]) for i, (src, dst) in enumerate(pairs)
    ]

    def frame_load(f):
        return pltpu.make_async_copy(video.at[0, f], vbuf.at[f], in_sem.at[f])

    query_loads = [
        pltpu.make_async_copy(queries, qall.at[me_d], q_sem.at[0]),
        pltpu.make_async_copy(qlen_in, qlen, q_sem.at[1]),
        pltpu.make_async_copy(qpos_in, qpos, q_sem.at[2]),
    ]
    frame_load(0).start()
    for i in range(first + 1):
        loads[i].start()
    for load in query_loads:
        load.start()
    for f in range(1, frames):
        frame_load(f).start()
    for i in range(first + 1, first + 4):
        loads[i].start()

    barrier = pltpu.get_barrier_semaphore()
    others = [(k, c) for k in range(nd) for c in range(ns) if k + c > 0]
    for k, c in others:
        pl.semaphore_signal(
            barrier, inc=1, device_id={"dp": ahead("dp", k), "seq": ahead("seq", c)},
            device_id_type=pl.DeviceIdType.MESH,
        )

    lane128 = lax.broadcasted_iota(jnp.int32, (1, 128), 1)
    low = (lane128 < 64).astype(F32).astype(BF16)
    high = (lane128 >= 64).astype(F32).astype(BF16)
    ra = lax.broadcasted_iota(jnp.int32, (CHUNK, CHUNK), 0) // 64
    ca = lax.broadcasted_iota(jnp.int32, (CHUNK, CHUNK), 1) // 64
    same_head = (ra == ca).astype(F32).astype(BF16)
    rm = lax.broadcasted_iota(jnp.int32, (rows, rows), 0) % PG
    cm = lax.broadcasted_iota(jnp.int32, (rows, rows), 1) % PG
    mask[...] = (rm == cm).astype(F32).astype(BF16)

    def query_copy(k):
        return remote(qall.at[me_d], qall.at[me_d], qs_sem.at[k - 1], qr_sem.at[k - 1], "dp", ahead("dp", k))

    def meta_copy(k):
        return remote(meta.at[me_d], meta.at[me_d], ms_sem.at[k - 1], mr_sem.at[k - 1], "dp", ahead("dp", k))

    lead = max(1, groups // 2)
    order = range(1, ns)

    def rows_copy(f, k):
        peer = ahead("seq", k)
        return remote(
            obuf.at[f, pl.ds(peer * groups, lead)], recv.at[pl.ds(0, lead), me_s, f],
            as_sem.at[f, k - 1], ar_sem.at[f, k - 1], "seq", peer,
        )

    def group_copy(g, k):
        peer = ahead("seq", k)
        return remote(
            obuf.at[:, peer * groups + g], recv.at[g, me_s],
            bs_sem.at[g - lead, k - 1], br_sem.at[g - lead, k - 1], "seq", peer,
        )

    def spatial(f, first_time):
        frame_load(f).wait()
        normed = layer_norm(vbuf[f].astype(F32))

        def ready(c):
            if first_time:
                for third in range(3):
                    loads[3 * c + third].wait()

        def put(c, value):
            bl[:, CHUNK * c:CHUNK * c + CHUNK] = value

        attend(normed, sq, same_head, low, high, None, ready, put)

    def spatial_out(f):
        for c in range(chunks):
            at = CHUNK * c
            update = dot(bl[...], so[:, at:at + CHUNK])
            obuf[f, :, :, at:at + CHUNK] = (
                vbuf[f, :, at:at + CHUNK].astype(F32) + update
            ).astype(BF16).reshape(patches // PG, PG, CHUNK)
        for k in reversed(order):
            rows_copy(f, k).start()

    spatial(0, True)
    loads[first].wait()
    pl.semaphore_wait(barrier, nd * ns - 1)
    spatial_out(0)
    for load in query_loads:
        load.wait()
    for k in range(1, nd):
        query_copy(k).start()
    per = 128 // lq
    tile = []
    for source in (qlen, qpos):
        for r in range(mrows):
            row = jnp.zeros((1, 128), jnp.int32)
            for c in range(per):
                row = jnp.where(lane128 // lq == c, source[r * per + c], row)
            tile.append(row)
    tile.append(jnp.zeros((8 - 2 * mrows, 128), jnp.int32))
    meta[me_d] = jnp.concatenate(tile, axis=0)
    for k in range(1, nd):
        meta_copy(k).start()

    @pl.loop(1, frames)
    def _(f):
        spatial(f, False)
        spatial_out(f)

    line = me_s // (ns // 4)
    inner = (line == 1) | (line == 2)
    late = [k for k in order if k >= ns // 2]
    soon = [k for k in order if not (k >= ns // 2)]
    for g in range(lead, groups):
        for k in soon:
            group_copy(g, k).start()

    @pl.when(jnp.logical_not(inner))
    def _():
        for g in range(lead, groups):
            for k in late:
                group_copy(g, k).start()

    for g in range(groups):
        recv[g, me_s] = obuf[:, me_s * groups + g]

    for k in range(1, nd):
        query_copy(k).wait()
        meta_copy(k).wait()
    for d in range(nd):
        qf = qall[d].astype(F32).T
        norm = lax.rsqrt(jnp.sum(qf * qf, axis=0, keepdims=True) + 1e-06)
        qht[:, d * qb:(d + 1) * qb] = (qf * norm).astype(BF16)
    sums[...] = jnp.zeros_like(sums)
    qs[...] = jnp.zeros_like(qs)
    for i in range(first + 1, first + 4):
        loads[i].wait()
    for f in range(frames):
        for k in order:
            rows_copy(f, k).wait_recv()

    def gather_queries(g):
        key = kh[g]
        for c in range(qt // CHUNK):
            cols = slice(CHUNK * c, CHUNK * c + CHUNK)
            qs[:, cols] += dot_tn(key, ebuf[g, :, cols])

    @pl.loop(0, groups)
    def _(g):
        @pl.when(g > 0)
        def _():
            gather_queries(g - 1)

        @pl.when(jnp.logical_and(inner, jnp.logical_and(g >= 0, g + lead < groups)))
        def _():
            for k in late:
                group_copy(g + lead, k).start()

        @pl.when(g >= lead)
        def _():
            for k in order:
                group_copy(g, k).wait_recv()

        x = recv[g].astype(F32).reshape(rows, width)
        normed = layer_norm(x)

        def put(c, value):
            bl2[:, CHUNK * c:CHUNK * c + CHUNK] = value

        attend(normed, tq, same_head, low, high, mask[...], lambda c: None, put)
        mixed = x + dot(bl2[...], to[...])
        normed = layer_norm(mixed.astype(BF16).astype(F32))
        proj = dot(normed, pw[...])
        key = (proj * lax.rsqrt(jnp.sum(proj * proj, axis=-1, keepdims=True) + 1e-06)).astype(BF16)
        kh[g] = key

        for c in range(qt // CHUNK):
            cols = slice(CHUNK * c, CHUNK * c + CHUNK)
            e = jnp.exp2(dot(key, qht[:, cols]) * (LOG2E / TEMPER) - LOG2E / TEMPER)
            sums[:, cols] += jnp.sum(e, axis=0, keepdims=True)
            ebuf[g, :, cols] = e.astype(BF16)

    for d in range(nd):
        for r in range(mrows):
            at = d * qb + 128 * r
            srecv[me_s, d, r:r + 1, :] = sums[:, at:at + 128]

    def sums_copy(k):
        return remote(srecv.at[me_s], srecv.at[me_s], ss_sem.at[k - 1], sr_sem.at[k - 1], "seq", ahead("seq", k))

    def block_sums_copy(k, c):
        i = (k - 1) * ns + c
        peer_d = ahead("dp", k)
        return pltpu.make_async_remote_copy(
            src_ref=srecv.at[me_s, peer_d], dst_ref=xrecv.at[me_d, me_s],
            send_sem=xs_sem.at[i], recv_sem=xr_sem.at[i],
            device_id={"dp": peer_d, "seq": ahead("seq", c)}, device_id_type=pl.DeviceIdType.MESH,
        )

    for k in range(nd - 1, 0, -1):
        for c in range(ns - 1, -1, -1):
            block_sums_copy(k, c).start()
    for k in range(ns - 1, 0, -1):
        sums_copy(k).start()

    gather_queries(groups - 1)
    for d in range(nd):
        part[d] = qs[:, d * qb:(d + 1) * qb].T.astype(BF16).reshape(2, qb // 2, 128)
    me_c = me_s % 2
    me_z = me_s // 2
    prec[me_d, me_c] = part[me_d, me_c]
    near = [(k, c) for k in range(nd) for c in range(2) if k + c > 0]

    def part_copy(i):
        k, c = near[i]
        peer_d = ahead("dp", k)
        peer_s = ahead("seq", c)
        return pltpu.make_async_remote_copy(
            src_ref=part.at[peer_d, peer_s % 2], dst_ref=prec.at[me_d, me_c],
            send_sem=ps_sem.at[i], recv_sem=pr_sem.at[i],
            device_id={"dp": peer_d, "seq": peer_s}, device_id_type=pl.DeviceIdType.MESH,
        )

    for i in range(len(near)):
        part_copy(i).start()

    seg_a = lax.broadcasted_iota(jnp.int32, (128, 128), 0) // lq
    seg_b = lax.broadcasted_iota(jnp.int32, (128, 128), 1) // lq
    seg = (seg_a == seg_b).astype(F32)
    slot = lax.broadcasted_iota(jnp.int32, (1, 128), 1) % lq

    def pair_terms(total, lens, hit):
        valid = (slot < lens).astype(F32)
        count = lens.astype(F32)
        smooth = (1.0 + TEMPER * jnp.log(total)) * valid
        score = jnp.dot(smooth, seg, precision=lax.Precision.HIGHEST, preferred_element_type=F32) / count
        sign = jnp.where(hit, 1.0, -1.0)
        margin = sign * (SLOPE * score + OFFSET)
        coeff = -sign * SLOPE / (1.0 + jnp.exp(margin)) * valid / count
        return margin, coeff / total

    for k in range(1, ns):
        sums_copy(k).wait()
    for k in range(1, nd):
        for c in range(ns):
            block_sums_copy(k, c).wait()
    for s in range(ns):
        xrecv[me_d, s] = srecv[s, me_d]
    block_total = []
    for d in range(nd):
        total = xrecv[d, 0]
        for s in range(1, ns):
            total = total + xrecv[d, s]
        block_total.append(total)
    block_total = jnp.concatenate(block_total, axis=0)
    block_len = jnp.concatenate([meta[me_d, :mrows]] * nd, axis=0)
    block_pos = jnp.concatenate([meta[me_d, mrows:2 * mrows]] * nd, axis=0)
    block_video = lax.broadcasted_iota(jnp.int32, (nd * mrows, 128), 0) // mrows
    _, block_scale = pair_terms(block_total, block_len, block_pos == block_video)
    half = mrows // 2
    tall = block_scale.T
    for i in range(len(near)):
        part_copy(i).wait()
    pieces = []
    for h in range(half):
        acc = jnp.zeros((128, 128), F32)
        for d in range(nd):
            at = d * mrows + h
            weight = jnp.where(me_c == 0, tall[:, at:at + 1], tall[:, at + half:at + half + 1])
            both = prec[d, 0, 128 * h:128 * h + 128].astype(F32) + prec[d, 1, 128 * h:128 * h + 128].astype(F32)
            acc = acc + both * weight
        pieces.append(acc.astype(BF16))
    zrec[me_z] = jnp.concatenate(pieces, axis=0)

    def chip_copy(k):
        return remote(zrec.at[me_z], zrec.at[me_z], rs_sem.at[k - 1], rr_sem.at[k - 1], "seq", ahead("seq", 2 * k))

    for k in range(1, ns // 2):
        chip_copy(k).start()

    trows = qt // 128
    total = []
    for d in range(nd):
        rows_d = srecv[0, d]
        for s in range(1, ns):
            rows_d = rows_d + srecv[s, d]
        total.append(rows_d)
    total = jnp.concatenate(total, axis=0)
    all_len = jnp.concatenate([meta[d, :mrows] for d in range(nd)], axis=0)
    all_pos = jnp.concatenate([meta[d, mrows:2 * mrows] for d in range(nd)], axis=0)
    margin, scale = pair_terms(total, all_len, all_pos == me_d)
    wrow = jnp.concatenate([scale[r:r + 1] for r in range(trows)], axis=1)
    wq = (qht[...].astype(F32) * wrow).astype(BF16)

    def grad_out(b):
        cols = pl.ds(16 * b, 16)
        return pltpu.make_async_copy(vgbuf.at[0, :, cols, :], vg.at[0, :, cols, :], v_sem.at[b])

    for b in range(ploc // 16):
        halves = [
            (dot_nt(ebuf[2 * b + h], wq) * float(fall * patches)).reshape(fall, PG, 128)
            for h in range(2)
        ]
        vgbuf[0, :, 16 * b:16 * b + 16, :] = jnp.concatenate(halves, axis=1).astype(BF16)
        grad_out(b).start()

    tail = jnp.exp(-jnp.abs(margin))
    losses = jnp.maximum(-margin, 0.0) + jnp.log1p(tail)
    nq = qt // lq
    lr = lax.broadcasted_iota(jnp.int32, (128, nq), 0)
    lc = lax.broadcasted_iota(jnp.int32, (128, nq), 1)
    pick = (lr == lc % per * lq).astype(F32)
    spread = jnp.dot(losses, pick, precision=lax.Precision.HIGHEST, preferred_element_type=F32)
    qr = lax.broadcasted_iota(jnp.int32, (trows, nq), 0)
    qc = lax.broadcasted_iota(jnp.int32, (trows, nq), 1) // per
    loss[...] = jnp.sum(jnp.where(qr == qc, spread, 0.0), axis=0, keepdims=True)

    for k in range(1, ns // 2):
        chip_copy(k).wait()
    acc = zrec[0].astype(F32)
    for z in range(1, ns // 2):
        acc = acc + zrec[z].astype(F32)
    gath[me_c] = (acc * float(lq)).astype(BF16)
    swap = remote(gath.at[me_c], gath.at[me_c], gs_sem.at[0], gr_sem.at[0], "seq", ahead("seq", 1))
    swap.start()
    swap.wait()
    qg[...] = gath[...].reshape(qg.shape)
    for b in range(ploc // 16):
        grad_out(b).wait()

    @pl.loop(0, frames)
    def _(f):
        for k in range(1, ns):
            rows_copy(f, k).wait_send()

    for g in range(lead, groups):
        for k in order:
            group_copy(g, k).wait_send()


def finish(vg_in, qg_in, loss_in, vg_out, qg_out, loss_out, vg_buf, qg_buf, loss_buf, in_sem, out_sem):
    steps = ((vg_in, vg_buf, vg_out), (qg_in, qg_buf, qg_out), (loss_in, loss_buf, loss_out))
    fetch = [pltpu.make_async_copy(a, b, in_sem.at[i]) for i, (a, b, _) in enumerate(steps)]
    store = [pltpu.make_async_copy(b, c, out_sem.at[i]) for i, (_, b, c) in enumerate(steps)]
    for copy in fetch:
        copy.start()
    for i in range(len(steps)):
        fetch[i].wait()
        store[i].start()
    for copy in store:
        copy.wait()


def body(nd, ns, video, space_qkv, space_out, time_qkv, time_out, proj_weight, queries, query_len, positive):
    videos_dev, frames, patches, width = video.shape
    assert videos_dev == 1
    qdev, lq, embed = queries.shape
    ploc = patches // ns
    fall = frames * ns
    rows = fall * PG
    groups = ploc // PG
    qb = qdev * lq
    qt = nd * qb
    vmem = pltpu.VMEM
    dma = pltpu.SemaphoreType.DMA
    anyspec = pl.BlockSpec(memory_space=pl.ANY)
    vspec = pl.BlockSpec(memory_space=pltpu.VMEM)
    vg, qg, loss = pl.pallas_call(
        functools.partial(kernel, nd, ns, lq),
        out_shape=(
            jax.ShapeDtypeStruct((1, fall, ploc, embed), BF16),
            jax.ShapeDtypeStruct((qdev, lq, embed), BF16),
            jax.ShapeDtypeStruct((1, nd * qdev), F32),
        ),
        in_specs=[anyspec] * 9,
        out_specs=(anyspec, vspec, vspec),
        scratch_shapes=[
            vmem((frames, patches, width), BF16),
            vmem(space_qkv.shape, BF16),
            vmem(space_out.shape, BF16),
            vmem(time_qkv.shape, BF16),
            vmem(time_out.shape, BF16),
            vmem(proj_weight.shape, BF16),
            vmem((frames, patches // PG, PG, width), BF16),
            vmem((patches, width), BF16),
            vmem((groups, ns, frames, PG, width), BF16),
            vmem((rows, width), BF16),
            vmem((rows, rows), BF16),
            vmem((groups, rows, embed), BF16),
            vmem((groups, rows, qt), BF16),
            vmem((1, qt), F32),
            vmem((embed, qt), F32),
            vmem((nd, qb, embed), BF16),
            vmem((nd, 8, 128), jnp.int32),
            vmem((ns, nd, qb // 128, 128), F32),
            vmem((nd, ns, qb // 128, 128), F32),
            vmem((nd, 2, qb // 2, embed), BF16),
            vmem((nd, 2, qb // 2, embed), BF16),
            vmem((ns // 2, qb // 2, embed), BF16),
            vmem((2, qb // 2, embed), BF16),
            vmem((embed, qt), BF16),
            vmem((1, fall, ploc, embed), BF16),
            pltpu.SMEM((qdev,), jnp.int32),
            pltpu.SMEM((qdev,), jnp.int32),
            dma((frames,)), dma((3 * (width // CHUNK) + 4,)),
            dma((3,)), dma((ploc // 16,)),
            dma((frames, ns - 1)), dma((frames, ns - 1)),
            dma((max(1, groups - groups // 2), ns - 1)), dma((max(1, groups - groups // 2), ns - 1)),
            dma((nd - 1,)), dma((nd - 1,)),
            dma((nd - 1,)), dma((nd - 1,)),
            dma((ns - 1,)), dma((ns - 1,)),
            dma(((nd - 1) * ns,)), dma(((nd - 1) * ns,)),
            dma((2 * nd - 1,)), dma((2 * nd - 1,)),
            dma((ns // 2 - 1,)), dma((ns // 2 - 1,)),
            dma((1,)), dma((1,)),
        ],
        compiler_params=pltpu.CompilerParams(
            collective_id=0, has_side_effects=True, vmem_limit_bytes=60 * 1024 * 1024
        ),
    )(
        video, space_qkv, space_out, time_qkv, time_out, proj_weight,
        queries.reshape(qb, embed), query_len, positive,
    )
    vg, qg, loss = pl.pallas_call(
        finish,
        out_shape=(
            jax.ShapeDtypeStruct(vg.shape, BF16),
            jax.ShapeDtypeStruct(qg.shape, BF16),
            jax.ShapeDtypeStruct(loss.shape, F32),
        ),
        in_specs=[anyspec] * 3,
        out_specs=(anyspec, anyspec, anyspec),
        scratch_shapes=[
            vmem(vg.shape, BF16), vmem(qg.shape, BF16), vmem(loss.shape, F32), dma((3,)), dma((3,)),
        ],
    )(vg, qg, loss)
    return vg, qg, loss.reshape(nd * qdev, 1)


def solution(mesh):
    nd, ns = mesh.shape["dp"], mesh.shape["seq"]
    placed = (
        P("dp", "seq", None, None),
        P(), P(), P(), P(), P(),
        P("dp", None, None),
        P("dp"),
        P("dp"),
    )
    return jax.shard_map(
        functools.partial(body, nd, ns),
        mesh=mesh,
        in_specs=placed,
        out_specs=(P("dp", None, "seq", None), P("dp", None, None), P(None, "dp")),
        check_vma=False,
    )
```

```python
import functools

import jax
import jax.numpy as jnp
from jax import lax
from jax.experimental import pallas as pl
from jax.experimental.pallas import tpu as pltpu
from jax.sharding import PartitionSpec as P

HEADS = 12
TEMPER = 0.05
SLOPE = 10.0
OFFSET = -5.0
SHARP = 10.0
LOG2E = 1.4426950408889634
CHUNK = 256
PG = 8
F32 = jnp.float32
BF16 = jnp.bfloat16


def dot(a, b):
    return jnp.dot(a, b, preferred_element_type=F32)


def dot_nt(a, b):
    return lax.dot_general(a, b, (((1,), (1,)), ((), ())), preferred_element_type=F32)


def dot_tn(a, b):
    return lax.dot_general(a, b, (((0,), (0,)), ((), ())), preferred_element_type=F32)


def layer_norm(values):
    center = values - jnp.mean(values, axis=-1, keepdims=True)
    spread = jnp.mean(center * center, axis=-1, keepdims=True)
    return (center * lax.rsqrt(spread + 1e-05)).astype(BF16)


def head_unit(values, same_head, scale):
    total = dot((values * values).astype(BF16), same_head)
    return values * (lax.rsqrt(total + 1e-06) * scale)


def scores(qn, kn, low, high, mask):
    out = []
    for p in range(CHUNK // 128):
        cols = slice(128 * p, 128 * p + 128)
        for half in (low, high):
            e = jnp.exp2(dot_nt(qn[:, cols] * half, kn[:, cols])).astype(BF16)
            if mask is not None:
                e = e * mask
            out.append(e)
    return out


def mix(weights, v):
    rows = v.shape[0]
    lane = lax.broadcasted_iota(jnp.int32, (rows, 128), 1) < 64
    ones = jnp.ones((rows, 128), BF16)
    out = []
    for p in range(CHUNK // 128):
        vx = jnp.concatenate([v[:, 128 * p:128 * p + 128], ones], axis=1)
        res = [dot(weights[2 * p + h], vx) for h in range(2)]
        num = jnp.where(lane, res[0][:, :128], res[1][:, :128])
        den = jnp.where(lane, res[0][:, 128:], res[1][:, 128:])
        out.append((num / den).astype(BF16))
    return jnp.concatenate(out, axis=1)


def attend(normed, w, same_head, low, high, mask, ready, put):
    width = normed.shape[1]
    chunks = width // CHUNK

    def project(c):
        ready(c)
        at = CHUNK * c
        q = dot(normed, w[:, at:at + CHUNK])
        k = dot(normed, w[:, width + at:width + at + CHUNK])
        v = dot(normed, w[:, 2 * width + at:2 * width + at + CHUNK]).astype(BF16)
        return q, k, v

    def unit(q, k):
        qn = head_unit(q, same_head, SHARP * LOG2E).astype(BF16)
        return qn, head_unit(k, same_head, 1.0).astype(BF16)

    q, k, v = project(0)
    qn, kn = unit(q, k)
    for c in range(chunks):
        now = v
        if c + 1 < chunks:
            q, k, v = project(c + 1)
        weights = scores(qn, kn, low, high, mask)
        if c + 1 < chunks:
            qn, kn = unit(q, k)
        put(c, mix(weights, now))


def kernel(
    nd, ns, lq,
    video, w_sq, w_so, w_tq, w_to, w_p, queries, qlen_in, qpos_in,
    vg, qg, loss,
    vbuf, sq, so, tq, to, pw, obuf, bl, recv, bl2, mask, kh, ebuf, sums, qs,
    qall, meta, srecv, xrecv, part, prec, zrec, gath, qht, vgbuf, lossbuf, qlen, qpos,
    in_sem, w_sem, q_sem, v_sem, o_sem, as_sem, ar_sem, bs_sem, br_sem, qs_sem, qr_sem, ms_sem, mr_sem, ss_sem, sr_sem,
    xs_sem, xr_sem, ps_sem, pr_sem, rs_sem, rr_sem, gs_sem, gr_sem,
):
    frames, patches, width = vbuf.shape
    ploc = patches // ns
    fall = frames * ns
    rows = fall * PG
    groups = ploc // PG
    chunks = width // CHUNK
    qb = qall.shape[1]
    qt = nd * qb
    mrows = qb // 128
    me_d = lax.axis_index("dp")
    me_s = lax.axis_index("seq")

    def ahead(axis, k):
        if axis == "dp":
            return lax.rem(me_d + k, nd)
        peer, bit = 0, 1
        while bit < ns:
            digit = (me_s // bit) % 2
            peer = peer + bit * (1 - digit if k & bit else digit)
            bit *= 2
        return peer

    def remote(src, dst, send, recv_at, axis, peer):
        return pltpu.make_async_remote_copy(
            src_ref=src, dst_ref=dst, send_sem=send, recv_sem=recv_at,
            device_id={axis: peer}, device_id_type=pl.DeviceIdType.MESH,
        )

    pairs = []
    for c in range(chunks):
        for third in range(3):
            cols = pl.ds(third * width + CHUNK * c, CHUNK)
            pairs.append((w_sq.at[:, cols], sq.at[:, cols]))
    first = len(pairs)
    pairs += [(w_so, so), (w_tq, tq), (w_to, to), (w_p, pw)]
    loads = [
        pltpu.make_async_copy(src, dst, w_sem.at[i]) for i, (src, dst) in enumerate(pairs)
    ]

    def frame_load(f):
        return pltpu.make_async_copy(video.at[0, f], vbuf.at[f], in_sem.at[f])

    query_loads = [
        pltpu.make_async_copy(queries, qall.at[me_d], q_sem.at[0]),
        pltpu.make_async_copy(qlen_in, qlen, q_sem.at[1]),
        pltpu.make_async_copy(qpos_in, qpos, q_sem.at[2]),
    ]
    frame_load(0).start()
    for i in range(first + 1):
        loads[i].start()
    for load in query_loads:
        load.start()
    for f in range(1, frames):
        frame_load(f).start()
    for i in range(first + 1, first + 4):
        loads[i].start()

    barrier = pltpu.get_barrier_semaphore()
    others = [(k, c) for k in range(nd) for c in range(ns) if k + c > 0]
    for k, c in others:
        pl.semaphore_signal(
            barrier, inc=1, device_id={"dp": ahead("dp", k), "seq": ahead("seq", c)},
            device_id_type=pl.DeviceIdType.MESH,
        )

    lane128 = lax.broadcasted_iota(jnp.int32, (1, 128), 1)
    low = (lane128 < 64).astype(F32).astype(BF16)
    high = (lane128 >= 64).astype(F32).astype(BF16)
    ra = lax.broadcasted_iota(jnp.int32, (CHUNK, CHUNK), 0) // 64
    ca = lax.broadcasted_iota(jnp.int32, (CHUNK, CHUNK), 1) // 64
    same_head = (ra == ca).astype(F32).astype(BF16)
    rm = lax.broadcasted_iota(jnp.int32, (rows, rows), 0) % PG
    cm = lax.broadcasted_iota(jnp.int32, (rows, rows), 1) % PG
    mask[...] = (rm == cm).astype(F32).astype(BF16)

    def query_copy(k):
        return remote(qall.at[me_d], qall.at[me_d], qs_sem.at[k - 1], qr_sem.at[k - 1], "dp", ahead("dp", k))

    def meta_copy(k):
        return remote(meta.at[me_d], meta.at[me_d], ms_sem.at[k - 1], mr_sem.at[k - 1], "dp", ahead("dp", k))

    lead = max(1, groups // 2)
    order = range(1, ns)

    def rows_copy(f, k):
        peer = ahead("seq", k)
        return remote(
            obuf.at[f, pl.ds(peer * groups, lead)], recv.at[pl.ds(0, lead), me_s, f],
            as_sem.at[f, k - 1], ar_sem.at[f, k - 1], "seq", peer,
        )

    def group_copy(g, k):
        peer = ahead("seq", k)
        return remote(
            obuf.at[:, peer * groups + g], recv.at[g, me_s],
            bs_sem.at[g - lead, k - 1], br_sem.at[g - lead, k - 1], "seq", peer,
        )

    def spatial(f, first_time):
        frame_load(f).wait()
        normed = layer_norm(vbuf[f].astype(F32))

        def ready(c):
            if first_time:
                for third in range(3):
                    loads[3 * c + third].wait()

        def put(c, value):
            bl[:, CHUNK * c:CHUNK * c + CHUNK] = value

        attend(normed, sq, same_head, low, high, None, ready, put)

    def spatial_out(f):
        for c in range(chunks):
            at = CHUNK * c
            update = dot(bl[...], so[:, at:at + CHUNK])
            obuf[f, :, :, at:at + CHUNK] = (
                vbuf[f, :, at:at + CHUNK].astype(F32) + update
            ).astype(BF16).reshape(patches // PG, PG, CHUNK)
        for k in reversed(order):
            rows_copy(f, k).start()

    spatial(0, True)
    loads[first].wait()
    pl.semaphore_wait(barrier, nd * ns - 1)
    spatial_out(0)
    for load in query_loads:
        load.wait()
    for k in range(1, nd):
        query_copy(k).start()
    per = 128 // lq
    tile = []
    for source in (qlen, qpos):
        for r in range(mrows):
            row = jnp.zeros((1, 128), jnp.int32)
            for c in range(per):
                row = jnp.where(lane128 // lq == c, source[r * per + c], row)
            tile.append(row)
    tile.append(jnp.zeros((8 - 2 * mrows, 128), jnp.int32))
    meta[me_d] = jnp.concatenate(tile, axis=0)
    for k in range(1, nd):
        meta_copy(k).start()

    @pl.loop(1, frames)
    def _(f):
        spatial(f, False)
        spatial_out(f)

    line = me_s // (ns // 4)
    inner = (line == 1) | (line == 2)
    late = [k for k in order if k >= ns // 2]
    soon = [k for k in order if not (k >= ns // 2)]
    for g in range(lead, groups):
        for k in soon:
            group_copy(g, k).start()

    @pl.when(jnp.logical_not(inner))
    def _():
        for g in range(lead, groups):
            for k in late:
                group_copy(g, k).start()

    for g in range(groups):
        recv[g, me_s] = obuf[:, me_s * groups + g]

    for k in range(1, nd):
        query_copy(k).wait()
        meta_copy(k).wait()
    for d in range(nd):
        qf = qall[d].astype(F32).T
        norm = lax.rsqrt(jnp.sum(qf * qf, axis=0, keepdims=True) + 1e-06)
        qht[:, d * qb:(d + 1) * qb] = (qf * norm).astype(BF16)
    sums[...] = jnp.zeros_like(sums)
    qs[...] = jnp.zeros_like(qs)
    for i in range(first + 1, first + 4):
        loads[i].wait()
    for f in range(frames):
        for k in order:
            rows_copy(f, k).wait_recv()

    def gather_queries(g):
        key = kh[g]
        for c in range(qt // CHUNK):
            cols = slice(CHUNK * c, CHUNK * c + CHUNK)
            qs[:, cols] += dot_tn(key, ebuf[g, :, cols])

    @pl.loop(0, groups)
    def _(g):
        @pl.when(g > 0)
        def _():
            gather_queries(g - 1)

        @pl.when(jnp.logical_and(inner, jnp.logical_and(g >= 0, g + lead < groups)))
        def _():
            for k in late:
                group_copy(g + lead, k).start()

        @pl.when(g >= lead)
        def _():
            for k in order:
                group_copy(g, k).wait_recv()

        x = recv[g].astype(F32).reshape(rows, width)
        normed = layer_norm(x)

        def put(c, value):
            bl2[:, CHUNK * c:CHUNK * c + CHUNK] = value

        attend(normed, tq, same_head, low, high, mask[...], lambda c: None, put)
        mixed = x + dot(bl2[...], to[...])
        normed = layer_norm(mixed.astype(BF16).astype(F32))
        proj = dot(normed, pw[...])
        key = (proj * lax.rsqrt(jnp.sum(proj * proj, axis=-1, keepdims=True) + 1e-06)).astype(BF16)
        kh[g] = key

        for c in range(qt // CHUNK):
            cols = slice(CHUNK * c, CHUNK * c + CHUNK)
            e = jnp.exp2(dot(key, qht[:, cols]) * (LOG2E / TEMPER) - LOG2E / TEMPER)
            sums[:, cols] += jnp.sum(e, axis=0, keepdims=True)
            ebuf[g, :, cols] = e.astype(BF16)

    for d in range(nd):
        for r in range(mrows):
            at = d * qb + 128 * r
            srecv[me_s, d, r:r + 1, :] = sums[:, at:at + 128]

    def sums_copy(k):
        return remote(srecv.at[me_s], srecv.at[me_s], ss_sem.at[k - 1], sr_sem.at[k - 1], "seq", ahead("seq", k))

    def block_sums_copy(k, c):
        i = (k - 1) * ns + c
        peer_d = ahead("dp", k)
        return pltpu.make_async_remote_copy(
            src_ref=srecv.at[me_s, peer_d], dst_ref=xrecv.at[me_d, me_s],
            send_sem=xs_sem.at[i], recv_sem=xr_sem.at[i],
            device_id={"dp": peer_d, "seq": ahead("seq", c)}, device_id_type=pl.DeviceIdType.MESH,
        )

    for k in range(nd - 1, 0, -1):
        for c in range(ns - 1, -1, -1):
            block_sums_copy(k, c).start()
    for k in range(ns - 1, 0, -1):
        sums_copy(k).start()

    gather_queries(groups - 1)
    for d in range(nd):
        part[d] = qs[:, d * qb:(d + 1) * qb].T.astype(BF16).reshape(2, qb // 2, 128)
    me_c = me_s % 2
    me_z = me_s // 2
    prec[me_d, me_c] = part[me_d, me_c]
    near = [(k, c) for k in range(nd) for c in range(2) if k + c > 0]

    def part_copy(i):
        k, c = near[i]
        peer_d = ahead("dp", k)
        peer_s = ahead("seq", c)
        return pltpu.make_async_remote_copy(
            src_ref=part.at[peer_d, peer_s % 2], dst_ref=prec.at[me_d, me_c],
            send_sem=ps_sem.at[i], recv_sem=pr_sem.at[i],
            device_id={"dp": peer_d, "seq": peer_s}, device_id_type=pl.DeviceIdType.MESH,
        )

    for i in range(len(near)):
        part_copy(i).start()

    seg_a = lax.broadcasted_iota(jnp.int32, (128, 128), 0) // lq
    seg_b = lax.broadcasted_iota(jnp.int32, (128, 128), 1) // lq
    seg = (seg_a == seg_b).astype(F32)
    slot = lax.broadcasted_iota(jnp.int32, (1, 128), 1) % lq

    def pair_terms(total, lens, hit):
        valid = (slot < lens).astype(F32)
        count = lens.astype(F32)
        smooth = (1.0 + TEMPER * jnp.log(total)) * valid
        score = jnp.dot(smooth, seg, precision=lax.Precision.HIGHEST, preferred_element_type=F32) / count
        sign = jnp.where(hit, 1.0, -1.0)
        margin = sign * (SLOPE * score + OFFSET)
        coeff = -sign * SLOPE / (1.0 + jnp.exp(margin)) * valid / count
        return margin, coeff / total

    for k in range(1, ns):
        sums_copy(k).wait()
    for k in range(1, nd):
        for c in range(ns):
            block_sums_copy(k, c).wait()
    for s in range(ns):
        xrecv[me_d, s] = srecv[s, me_d]
    block_total = []
    for d in range(nd):
        total = xrecv[d, 0]
        for s in range(1, ns):
            total = total + xrecv[d, s]
        block_total.append(total)
    block_total = jnp.concatenate(block_total, axis=0)
    block_len = jnp.concatenate([meta[me_d, :mrows]] * nd, axis=0)
    block_pos = jnp.concatenate([meta[me_d, mrows:2 * mrows]] * nd, axis=0)
    block_video = lax.broadcasted_iota(jnp.int32, (nd * mrows, 128), 0) // mrows
    _, block_scale = pair_terms(block_total, block_len, block_pos == block_video)
    half = mrows // 2
    tall = block_scale.T
    for i in range(len(near)):
        part_copy(i).wait()
    pieces = []
    for h in range(half):
        acc = jnp.zeros((128, 128), F32)
        for d in range(nd):
            at = d * mrows + h
            weight = jnp.where(me_c == 0, tall[:, at:at + 1], tall[:, at + half:at + half + 1])
            both = prec[d, 0, 128 * h:128 * h + 128].astype(F32) + prec[d, 1, 128 * h:128 * h + 128].astype(F32)
            acc = acc + both * weight
        pieces.append(acc.astype(BF16))
    zrec[me_z] = jnp.concatenate(pieces, axis=0)

    def chip_copy(k):
        return remote(zrec.at[me_z], zrec.at[me_z], rs_sem.at[k - 1], rr_sem.at[k - 1], "seq", ahead("seq", 2 * k))

    for k in range(1, ns // 2):
        chip_copy(k).start()

    trows = qt // 128
    total = []
    for d in range(nd):
        rows_d = srecv[0, d]
        for s in range(1, ns):
            rows_d = rows_d + srecv[s, d]
        total.append(rows_d)
    total = jnp.concatenate(total, axis=0)
    all_len = jnp.concatenate([meta[d, :mrows] for d in range(nd)], axis=0)
    all_pos = jnp.concatenate([meta[d, mrows:2 * mrows] for d in range(nd)], axis=0)
    margin, scale = pair_terms(total, all_len, all_pos == me_d)
    wrow = jnp.concatenate([scale[r:r + 1] for r in range(trows)], axis=1)
    wq = (qht[...].astype(F32) * wrow).astype(BF16)

    def grad_out(b):
        cols = pl.ds(16 * b, 16)
        return pltpu.make_async_copy(vgbuf.at[0, :, cols, :], vg.at[0, :, cols, :], v_sem.at[b])

    for b in range(ploc // 16):
        halves = [
            (dot_nt(ebuf[2 * b + h], wq) * float(fall * patches)).reshape(fall, PG, 128)
            for h in range(2)
        ]
        vgbuf[0, :, 16 * b:16 * b + 16, :] = jnp.concatenate(halves, axis=1).astype(BF16)
        grad_out(b).start()

    tail = jnp.exp(-jnp.abs(margin))
    losses = jnp.maximum(-margin, 0.0) + jnp.log1p(tail)
    nq = qt // lq
    lr = lax.broadcasted_iota(jnp.int32, (128, nq), 0)
    lc = lax.broadcasted_iota(jnp.int32, (128, nq), 1)
    pick = (lr == lc % per * lq).astype(F32)
    spread = jnp.dot(losses, pick, precision=lax.Precision.HIGHEST, preferred_element_type=F32)
    qr = lax.broadcasted_iota(jnp.int32, (trows, nq), 0)
    qc = lax.broadcasted_iota(jnp.int32, (trows, nq), 1) // per
    lossbuf[...] = jnp.sum(jnp.where(qr == qc, spread, 0.0), axis=0, keepdims=True)
    loss_out = pltpu.make_async_copy(lossbuf, loss, o_sem.at[0])
    loss_out.start()

    for k in range(1, ns // 2):
        chip_copy(k).wait()
    acc = zrec[0].astype(F32)
    for z in range(1, ns // 2):
        acc = acc + zrec[z].astype(F32)
    gath[me_c] = (acc * float(lq)).astype(BF16)
    swap = remote(gath.at[me_c], gath.at[me_c], gs_sem.at[0], gr_sem.at[0], "seq", ahead("seq", 1))
    swap.start()
    mine = pltpu.make_async_copy(gath.at[me_c], qg.at[me_c], o_sem.at[1])
    mine.start()
    swap.wait()
    other = pltpu.make_async_copy(gath.at[1 - me_c], qg.at[1 - me_c], o_sem.at[2])
    other.start()
    loss_out.wait()
    mine.wait()
    for b in range(ploc // 16):
        grad_out(b).wait()

    @pl.loop(0, frames)
    def _(f):
        for k in range(1, ns):
            rows_copy(f, k).wait_send()

    for g in range(lead, groups):
        for k in order:
            group_copy(g, k).wait_send()
    other.wait()


def finish(vg_in, qg_in, loss_in, vg_out, qg_out, loss_out, vg_buf, qg_buf, loss_buf, in_sem, out_sem):
    steps = ((vg_in, vg_buf, vg_out), (qg_in, qg_buf, qg_out), (loss_in, loss_buf, loss_out))
    fetch = [pltpu.make_async_copy(a, b, in_sem.at[i]) for i, (a, b, _) in enumerate(steps)]
    store = [pltpu.make_async_copy(b, c, out_sem.at[i]) for i, (_, b, c) in enumerate(steps)]
    for copy in fetch:
        copy.start()
    for i in range(len(steps)):
        fetch[i].wait()
        store[i].start()
    for copy in store:
        copy.wait()


def body(nd, ns, video, space_qkv, space_out, time_qkv, time_out, proj_weight, queries, query_len, positive):
    videos_dev, frames, patches, width = video.shape
    assert videos_dev == 1
    qdev, lq, embed = queries.shape
    ploc = patches // ns
    fall = frames * ns
    rows = fall * PG
    groups = ploc // PG
    qb = qdev * lq
    qt = nd * qb
    vmem = pltpu.VMEM
    dma = pltpu.SemaphoreType.DMA
    anyspec = pl.BlockSpec(memory_space=pl.ANY)
    vspec = pl.BlockSpec(memory_space=pltpu.VMEM)
    vg, qg, loss = pl.pallas_call(
        functools.partial(kernel, nd, ns, lq),
        out_shape=(
            jax.ShapeDtypeStruct((1, fall, ploc, embed), BF16),
            jax.ShapeDtypeStruct((2, qb // 2, embed), BF16),
            jax.ShapeDtypeStruct((1, nd * qdev), F32),
        ),
        in_specs=[anyspec] * 9,
        out_specs=(anyspec, anyspec, anyspec),
        scratch_shapes=[
            vmem((frames, patches, width), BF16),
            vmem(space_qkv.shape, BF16),
            vmem(space_out.shape, BF16),
            vmem(time_qkv.shape, BF16),
            vmem(time_out.shape, BF16),
            vmem(proj_weight.shape, BF16),
            vmem((frames, patches // PG, PG, width), BF16),
            vmem((patches, width), BF16),
            vmem((groups, ns, frames, PG, width), BF16),
            vmem((rows, width), BF16),
            vmem((rows, rows), BF16),
            vmem((groups, rows, embed), BF16),
            vmem((groups, rows, qt), BF16),
            vmem((1, qt), F32),
            vmem((embed, qt), F32),
            vmem((nd, qb, embed), BF16),
            vmem((nd, 8, 128), jnp.int32),
            vmem((ns, nd, qb // 128, 128), F32),
            vmem((nd, ns, qb // 128, 128), F32),
            vmem((nd, 2, qb // 2, embed), BF16),
            vmem((nd, 2, qb // 2, embed), BF16),
            vmem((ns // 2, qb // 2, embed), BF16),
            vmem((2, qb // 2, embed), BF16),
            vmem((embed, qt), BF16),
            vmem((1, fall, ploc, embed), BF16),
            vmem((1, nd * qdev), F32),
            pltpu.SMEM((qdev,), jnp.int32),
            pltpu.SMEM((qdev,), jnp.int32),
            dma((frames,)), dma((3 * (width // CHUNK) + 4,)),
            dma((3,)), dma((ploc // 16,)), dma((3,)),
            dma((frames, ns - 1)), dma((frames, ns - 1)),
            dma((max(1, groups - groups // 2), ns - 1)), dma((max(1, groups - groups // 2), ns - 1)),
            dma((nd - 1,)), dma((nd - 1,)),
            dma((nd - 1,)), dma((nd - 1,)),
            dma((ns - 1,)), dma((ns - 1,)),
            dma(((nd - 1) * ns,)), dma(((nd - 1) * ns,)),
            dma((2 * nd - 1,)), dma((2 * nd - 1,)),
            dma((ns // 2 - 1,)), dma((ns // 2 - 1,)),
            dma((1,)), dma((1,)),
        ],
        compiler_params=pltpu.CompilerParams(
            collective_id=0, has_side_effects=True, vmem_limit_bytes=60 * 1024 * 1024
        ),
    )(
        video, space_qkv, space_out, time_qkv, time_out, proj_weight,
        queries.reshape(qb, embed), query_len, positive,
    )
    vg, qg, loss = pl.pallas_call(
        finish,
        out_shape=(
            jax.ShapeDtypeStruct(vg.shape, BF16),
            jax.ShapeDtypeStruct(qg.shape, BF16),
            jax.ShapeDtypeStruct(loss.shape, F32),
        ),
        in_specs=[anyspec] * 3,
        out_specs=(anyspec, anyspec, anyspec),
        scratch_shapes=[
            vmem(vg.shape, BF16), vmem(qg.shape, BF16), vmem(loss.shape, F32), dma((3,)), dma((3,)),
        ],
    )(vg, qg, loss)
    return vg, qg.reshape(qdev, lq, embed), loss.reshape(nd * qdev, 1)


def solution(mesh):
    nd, ns = mesh.shape["dp"], mesh.shape["seq"]
    placed = (
        P("dp", "seq", None, None),
        P(), P(), P(), P(), P(),
        P("dp", None, None),
        P("dp"),
        P("dp"),
    )
    return jax.shard_map(
        functools.partial(body, nd, ns),
        mesh=mesh,
        in_specs=placed,
        out_specs=(P("dp", None, "seq", None), P("dp", None, None), P(None, "dp")),
        check_vma=False,
    )
```
